256 devices in a mesh: req: 32 (over z_lo, x, core), tp: 8 (over z_hi, y).
Axes of the slice: x: 4, y: 4, z: 8 (z_hi: 2, z_lo: 4; z = z_hi * 4 + z_lo), core: 2. Of those that a mesh axis runs over, the one named last changes fastest.
Arguments:
- hidden: bfloat16 [8192, 4608], P('req', 'tp'), may hold values from -6 to 6
- norm_gain: float32 [4608], replicated, may hold values from 0.1 to 1.9
- w_query: bfloat16 [4608, 4096], P(None, 'tp'), may hold values from -0.25 to 0.25
- w_key: bfloat16 [4608, 2048], P(None, 'tp'), may hold values from -0.09375 to 0.09375
- w_value: bfloat16 [4608, 2048], P(None, 'tp'), may hold values from -0.09375 to 0.09375
- prefix_kv: bfloat16 [16384, 2, 2048], P('req', None, 'tp'), may hold values from -6 to 6
- group_of: int32 [32], replicated, may hold values from 0 to 3, as said below
- block_owner: int32 [4, 8], replicated, may hold values from 0 to 31, as said below
- lengths: int32 [32], replicated, may hold values from 32 to 256, as said below
Outputs:
- attended: bfloat16 [8192, 4096], P('req', 'tp')
- key_cache: bfloat16 [8192, 2048], P('req', 'tp')
- value_cache: bfloat16 [8192, 2048], P('req', 'tp')
The draws below stay inside these ranges and needn't reach their ends.
Inputs may be any that keep to these rules, and one draw needn't show every extreme that they name: `group_of`: every group holds exactly 8 requests. `block_owner`: every block index appears exactly once. `lengths`: some request has exactly 256 live rows and some exactly 32.
All inputs are finite; a program needn't handle non-finite values.
Results may differ from the reference program's by a relative error of at most 0.011.
Values may be sent and summed in bfloat16 or wider, within the bound.
A program may use at most 256 MiB of HBM per device.

```python
import math
import jax
import jax.numpy as jnp
from jax import lax

D = 4608
QH = 32
KVH = 16
HD = 128
GSIZE = 8
SUF = 256
PRE_DEV = 512
REQUESTS = 32
GROUPS = 4
PREFIX = 4096
TOKENS = 8192


def draw_group_of(key, part):
    shuffled = jax.random.permutation(jax.random.fold_in(key, 11), REQUESTS)
    return (shuffled // GSIZE).astype(jnp.int32)


def draw_block_owner(key, part):
    shuffled = jax.random.permutation(jax.random.fold_in(key, 23), REQUESTS)
    return shuffled.astype(jnp.int32).reshape(GROUPS, GSIZE)


def draw_lengths(key, part):
    shortest = SUF // 8
    drawn = jax.random.randint(jax.random.fold_in(key, 31), (REQUESTS,), shortest, SUF + 1)
    chosen = jax.random.permutation(jax.random.fold_in(key, 37), REQUESTS)
    drawn = drawn.at[chosen[0]].set(SUF).at[chosen[1]].set(shortest)
    return drawn.astype(jnp.int32)


def levels(key, dims, pieces, low, largest):
    gain, own = 1.0, jax.random.fold_in(key, 6)
    for position, parts in pieces:
        steps = jnp.exp(jax.random.uniform(jax.random.fold_in(own, position), (parts,), jnp.float32, low / len(pieces), largest / len(pieces)))
        gain = gain * jnp.repeat(steps, dims[position] // parts).reshape([-1 if axis == position else 1 for axis in range(len(dims))])
    return gain


def gaussian(own_key, extent, spread, most, shards=(), held_as=jnp.bfloat16):
    values = jax.random.normal(own_key, extent, jnp.float32) * spread
    if len(shards) > 0:
        values = levels(own_key, extent, shards, -0.22, 0.18) * values
    return jnp.clip(values, min=-most, max=most).astype(held_as)


def setup_inputs(seed: int = 0) -> dict:
    arg_keys = jax.random.split(jax.random.key(seed), 10)
    hidden = gaussian(arg_keys[0], (TOKENS, D), 1.0, 6.0, ((0, 32), (1, 8)))
    norm_gain = jnp.clip(1.0 + 0.18 * jax.random.normal(arg_keys[1], (D,), jnp.float32), 0.1, 1.9)
    w_query = gaussian(arg_keys[2], (D, QH * HD), (D // 9) ** -0.5, 0.25, ((1, 8),))
    w_key = gaussian(arg_keys[3], (D, KVH * HD), D ** -0.5, 0.09375, ((1, 8),))
    w_value = gaussian(arg_keys[4], (D, KVH * HD), D ** -0.5, 0.09375, ((1, 8),))
    prefix_kv = gaussian(arg_keys[5], (REQUESTS * PRE_DEV, 2, KVH * HD), 1.0, 6.0, ((0, 32), (2, 8)))
    group_of = draw_group_of(jax.random.fold_in(arg_keys[9], 71), 0)
    block_owner = draw_block_owner(jax.random.fold_in(arg_keys[9], 71), 0)
    lengths = draw_lengths(jax.random.fold_in(arg_keys[9], 71), 0)
    return dict(hidden=hidden, norm_gain=norm_gain, w_query=w_query, w_key=w_key, w_value=w_value, prefix_kv=prefix_kv, group_of=group_of, block_owner=block_owner, lengths=lengths)


SOFTCAP = 50.0
EPSILON = 1e-06
QUERY_SCALE = 1.0 / 12.0

def rope_tables(positions, head_width):
    half_width = head_width // 2
    inverse_freq = jnp.exp(jnp.arange(half_width).astype(jnp.float32) * (-2.0 * math.log(10000.0) / head_width))
    angles = positions.astype(jnp.float32)[:, None] * inverse_freq[None, :]
    return (jnp.cos(angles), jnp.sin(angles))

def rotate(values, cosine_table, sine_table):
    half_width = values.shape[-1] // 2
    lower_half = values[..., :half_width]
    upper_half = values[..., half_width:]
    cosine_part = cosine_table[:, None, :]
    sine_part = sine_table[:, None, :]
    return jnp.concatenate([lower_half * cosine_part - upper_half * sine_part, upper_half * cosine_part + lower_half * sine_part], axis=-1)

def reference(hidden, norm_gain, w_query, w_key, w_value, prefix_kv, group_of, block_owner, lengths):
    row_total = REQUESTS * SUF
    features = hidden.astype(jnp.float32)
    row_scale = lax.rsqrt(lax.optimization_barrier(jnp.mean(features * features, axis=1, keepdims=True)) + EPSILON)
    normed = (features * row_scale * norm_gain[None, :]).astype(jnp.bfloat16)
    query_raw = jnp.dot(normed, w_query, preferred_element_type=jnp.float32)
    key_raw = jnp.dot(normed, w_key, preferred_element_type=jnp.float32)
    value_raw = jnp.dot(normed, w_value, preferred_element_type=jnp.float32)
    local_rows = jnp.arange(row_total) % SUF
    cosine_table, sine_table = rope_tables(local_rows + PREFIX, HD)
    query_rows = (rotate(query_raw.reshape(row_total, QH, HD), cosine_table, sine_table) * QUERY_SCALE).astype(jnp.bfloat16)
    request_of_row = jnp.arange(row_total) // SUF
    live_rows = local_rows < lengths[request_of_row]
    key_rows = jnp.where(live_rows[:, None, None], rotate(key_raw.reshape(row_total, KVH, HD), cosine_table, sine_table), 0.0).astype(jnp.bfloat16)
    value_rows = jnp.where(live_rows[:, None], value_raw, 0.0).astype(jnp.bfloat16)
    prefix_blocks = prefix_kv.reshape(REQUESTS, PRE_DEV, 2, KVH, HD)
    query_by_request = query_rows.reshape(REQUESTS, SUF, KVH, QH // KVH, HD)
    key_by_request = key_rows.reshape(REQUESTS, SUF, KVH, HD)
    value_by_request = value_rows.reshape(REQUESTS, SUF, KVH, HD)
    causal = jnp.arange(SUF)[:, None] >= jnp.arange(SUF)[None, :]
    allowed = jnp.concatenate([jnp.full((SUF, PREFIX), True), causal], axis=1)

    def one_request(request):
        blocks = prefix_blocks[block_owner[group_of[request]]].reshape(PREFIX, 2, KVH, HD)
        key_all = jnp.concatenate([blocks[:, 0], key_by_request[request]], axis=0).astype(jnp.float32)
        value_all = jnp.concatenate([blocks[:, 1], value_by_request[request]], axis=0).astype(jnp.float32)
        grouped = query_by_request[request].astype(jnp.float32)
        scores = jnp.einsum('rkgd,ckd->kgrc', grouped, key_all)
        weights = jnp.where(allowed[None, None], jnp.exp(SOFTCAP * jnp.tanh(scores / SOFTCAP)), 0.0)
        denominator = lax.optimization_barrier(jnp.sum(weights, axis=3))
        rounded = lax.optimization_barrier(weights.astype(jnp.bfloat16)).astype(jnp.float32)
        numerator = jnp.einsum('kgrc,ckd->rkgd', rounded, value_all)
        result = numerator / jnp.transpose(denominator, (2, 0, 1))[..., None]
        live_here = jnp.arange(SUF) < lengths[request]
        result = jnp.where(live_here[:, None, None, None], result, 0.0)
        return result.reshape(SUF, QH * HD).astype(jnp.bfloat16)
    attended = lax.map(one_request, jnp.arange(REQUESTS)).reshape(row_total, QH * HD)
    return (attended, key_rows.reshape(row_total, KVH * HD), value_rows)
```

```python
import functools
import math

import jax
import jax.numpy as jnp
import numpy as np
from jax import lax
from jax.experimental import pallas as pl
from jax.experimental.pallas import tpu as pltpu
from jax.sharding import PartitionSpec as P

MESH = pl.DeviceIdType.MESH
BF = jnp.bfloat16
F32 = jnp.float32
HD = 128
ROWS = 256
PREFIX = 4096
FEAT = 576
TP = 8
SL = 64
LOG2E = 1.4426950408889634


def rope_constants():
    freq = np.exp(np.arange(64, dtype=np.float32) * np.float32(-2.0 * math.log(10000.0) / 128))
    angle = (np.arange(ROWS) + PREFIX).astype(np.float32)[:, None] * freq[None, :]
    cosine, sine = np.cos(angle.astype(np.float64)), np.sin(angle.astype(np.float64))
    full_cos = np.concatenate([cosine, cosine], axis=1).astype(np.float32)
    signed_sin = np.concatenate([-sine, sine], axis=1).astype(np.float32)
    return full_cos, signed_sin


def kernel(
    group_ref, owner_ref, length_ref, hid, wq, wk, wv, kv, gain_ref, cos_ref, sin_ref,
    att_ref, key_ref, val_ref,
    hbuf, wbuf, kvb0, kvb1, qb0, qb1, ns0, ns1, nr0, nr1, ds0, ds1, dr0, dr1,
    acc, sq, gcol, kscr, vscr, snum, sden,
    lsem, wsem, qss, qsr, hs, hr, cs, cr, zs, zr, qs, qr, rs, rr, es, er,
):
    kvb, qb, ns, nr, ds, dr = (kvb0, kvb1), (qb0, qb1), (ns0, ns1), (nr0, nr1), (ds0, ds1), (dr0, dr1)
    me = lax.axis_index("req")
    t = lax.axis_index("tp")
    p, s = me // 8, me % 8
    c = s % 2
    zh, y = t // 4, t % 4
    inner = (p * (3 - p)) // 2
    mid = inner == 1
    zo = (p + 1 - 2 * (p % 2), 2 - p // 2, 3 - 3 * (p // 2))

    def row_dev(slot):
        return (p * 8 + slot, t)

    def z_dev(z):
        return (z * 8 + s, t)

    def tp_dev(other):
        return (me, other)

    def slot_at(rel):
        return (s + rel) % 8

    def copy_to(src, dst, send, recv, dev):
        return pltpu.make_async_remote_copy(src, dst, send, recv, device_id=dev, device_id_type=MESH)

    sibling = p * 8 + s + 1 - 2 * c
    partner = (1 - zh) * 4 + y
    ys = [(y + 1) % 4, (y + 3) % 4, (y + 2) % 4]
    yin = [(y + 3) % 4, (y + 1) % 4, (y + 2) % 4]

    own_hid = pltpu.make_async_copy(hid, hbuf.at[t], lsem.at[0])
    own_hid.start()
    own_kv = [
        pltpu.make_async_copy(kv.at[h, pl.ds(s * SL, SL)], kvb[h].at[me], lsem.at[1 + h])
        for h in range(2)
    ]
    loads = [
        pltpu.make_async_copy(wq, wbuf.at[:, 0:512], wsem.at[0]),
        pltpu.make_async_copy(wk, wbuf.at[:, 512:768], wsem.at[1]),
        pltpu.make_async_copy(wv, wbuf.at[:, 768:1024], wsem.at[2]),
    ]

    barrier = pltpu.get_barrier_semaphore()
    greet = [row_dev(slot_at(rel)) for rel in range(1, 8)]
    greet += [z_dev(zo[0])] + [tp_dev((t + i) % TP) for i in range(1, TP)]
    for dev in greet:
        pl.semaphore_signal(barrier, inc=1, device_id=dev, device_id_type=MESH)

    @pl.when(mid)
    def _():
        pl.semaphore_signal(barrier, inc=1, device_id=z_dev(3 - p), device_id_type=MESH)

    eye = lax.broadcasted_iota(jnp.int32, (HD, HD), 0) == lax.broadcasted_iota(jnp.int32, (HD, HD), 1)
    own_hid.wait()
    features = hbuf[t].astype(F32)
    sq[t] = jnp.broadcast_to(jnp.sum(features * features, axis=0, keepdims=True), (8, ROWS))
    pl.semaphore_wait(barrier, len(greet) + inner)

    pending = []

    def go(copy):
        copy.start()
        pending.append(copy)

    def sq_copy(i):
        return copy_to(sq.at[t], sq.at[t], qss.at[i], qsr.at[i], tp_dev((t + i) % TP))

    def sq_wait(i):
        ref = sq.at[(t + TP - i) % TP]
        copy_to(ref, ref, qss.at[i], qsr.at[i], tp_dev(t)).wait_recv()

    for i in range(1, TP):
        go(sq_copy(i))

    def hid_copy(i, src, holder, dev):
        return copy_to(src, hbuf.at[holder], hs.at[i], hr.at[i], tp_dev(dev))

    go(hid_copy(0, hid, t, partner))
    for i, o in enumerate(ys):
        go(hid_copy(1 + i, hid, t, zh * 4 + o))

    def scatter(h, rel):
        slot = slot_at(rel)
        src = kv.at[h, pl.ds(pl.multiple_of(slot * SL, SL), SL)]
        return copy_to(src, kvb[h].at[me], cs.at[h, rel], cr.at[h, rel], row_dev(slot))

    def scatter_wait(h, rel):
        ref = kvb[h].at[p * 8 + slot_at(8 - rel)]
        copy_to(ref, ref, cs.at[h, rel], cr.at[h, rel], row_dev(s)).wait_recv()

    for h in range(2):
        for rel in range(1, 8):
            go(scatter(h, rel))
        own_kv[h].start()
    for load in loads:
        load.start()

    def z_rows(h, z):
        return kvb[h].at[pl.ds(pl.multiple_of(z * 8, 8), 8)]

    def z_copy(h, k, which):
        if which == "first":
            ref, target, sem, at = z_rows(h, p), zo[0], 0, 0
        elif which == "second":
            ref, target, sem, at = z_rows(h, p), 3 - p, 1, 1
        else:
            ref, target, sem = z_rows(h, zo[k]), (3 - p if k == 0 else 3 * p - 3), 2 + k
            at = (2, 1, 2)[k]
        return copy_to(ref, ref, zs.at[h, sem], zr.at[h, at], z_dev(target))

    def z_own(h):
        for rel in range(1, 8):
            scatter_wait(h, rel)
        own_kv[h].wait()
        go(z_copy(h, 0, "first"))

        @pl.when(mid)
        def _():
            z_copy(h, 0, "second").start()

    def z_step(h, k):
        ref = z_rows(h, zo[k])
        copy_to(ref, ref, zs.at[h, 0], zr.at[h, k], z_dev(p)).wait_recv()

        @pl.when(mid)
        def _():
            z_copy(h, k, "relay").start()

    def hid_wait(i, holder):
        ref = hbuf.at[holder]
        copy_to(ref, ref, hs.at[i], hr.at[i], tp_dev(t)).wait_recv()

    acc[...] = jnp.zeros_like(acc)
    for i in range(TP * FEAT // HD):
        at = slice(i * HD, (i + 1) * HD)
        spread = jnp.where(eye, jnp.broadcast_to(gain_ref[:, at], (HD, HD)), 0.0)
        gcol[at, :] = jnp.broadcast_to(jnp.sum(spread, axis=1, keepdims=True), (HD, HD))

    def project(holder, row_scale):
        at = pl.ds(pl.multiple_of(holder * FEAT, FEAT), FEAT)
        gain = gcol[at, :]
        normed = hbuf[holder].astype(F32) * row_scale * jnp.concatenate([gain, gain], axis=1)
        acc[...] += lax.dot_general(
            normed.astype(BF), wbuf[at, :], (((0,), (0,)), ((), ())), preferred_element_type=F32
        )

    vscr[...] = jnp.ones_like(vscr)

    for load in loads:
        load.wait()
    for i in range(1, TP):
        sq_wait(i)
    total = sq[0]
    for i in range(1, TP):
        total = total + sq[i]
    row_scale = lax.rsqrt(total[0:1, :] / (TP * FEAT) + 1e-6)
    project(t, row_scale)
    hid_wait(0, partner)
    for i, o in enumerate(ys):
        go(hid_copy(4 + i, hbuf.at[partner], partner, zh * 4 + o))
    z_own(0)
    project(partner, row_scale)
    for i in range(3):
        hid_wait(1 + i, zh * 4 + yin[i])
        project(zh * 4 + yin[i], row_scale)
    z_step(0, 0)
    for i in range(3):
        hid_wait(4 + i, (1 - zh) * 4 + yin[i])
        project((1 - zh) * 4 + yin[i], row_scale)
    z_step(0, 1)
    z_own(1)

    cosine, sine = cos_ref[...], sin_ref[...]
    live = lax.broadcasted_iota(jnp.int32, (ROWS, HD), 0) < length_ref[me]

    def rotated(at):
        x = acc[:, at : at + HD]
        return x * cosine + pltpu.roll(x, 64, 1) * sine

    for h in range(2):
        for g in range(2):
            q = (rotated((2 * h + g) * HD) * (1.0 / 12.0)).astype(BF)
            qb[h][s, g * ROWS : (g + 1) * ROWS, :] = q
    for h in range(2):
        key_ref[:, h * HD : (h + 1) * HD] = jnp.where(live, rotated(512 + h * HD), 0.0).astype(BF)
        v = acc[:, 768 + h * HD : 768 + (h + 1) * HD]
        val_ref[:, h * HD : (h + 1) * HD] = jnp.where(live, v, 0.0).astype(BF)

    def q_copy(h, slot, sem, rel, dev):
        ref = qb[h].at[slot]
        return copy_to(ref, ref, qs.at[h, sem], qr.at[h, rel], dev)

    def q_wait(h, rel):
        ref = qb[h].at[slot_at(rel)]
        copy_to(ref, ref, qs.at[h, 0], qr.at[h, rel], row_dev(s)).wait_recv()

    def sib_rel(rel):
        return (rel + 2 * c + 7) % 8

    for h in range(2):
        for n, rel in enumerate((2, 6, 4)):
            go(q_copy(h, s, n, 8 - rel, row_dev(slot_at(rel))))
        go(q_copy(h, s, 3, sib_rel(0), (sibling, t)))

    def weigh(scores):
        return jnp.exp2(jnp.tanh(scores * (1.0 / 50.0)) * (50.0 * LOG2E))

    contract = (((1,), (1,)), ((), ()))
    row_id = lax.broadcasted_iota(jnp.int32, (2 * ROWS, ROWS), 0) % ROWS
    col_id = lax.broadcasted_iota(jnp.int32, (2 * ROWS, ROWS), 1)
    causal = row_id >= col_id
    ones = jnp.ones((ROWS, HD), BF)
    for h in range(2):
        scores = lax.dot_general(
            qb[h][s], key_ref[:, h * HD : (h + 1) * HD], contract, preferred_element_type=F32
        )
        w = jnp.where(causal, weigh(scores), 0.0).astype(BF)
        values = jnp.concatenate([val_ref[:, h * HD : (h + 1) * HD], ones], axis=1)
        both = jnp.dot(w, values, preferred_element_type=F32)
        snum[h] = both[:, :HD]
        sden[h] = both[:, HD:]
    z_step(0, 2)

    for h in range(2):
        for n, rel in enumerate((2, 6, 4)):
            q_wait(h, rel)
            go(q_copy(h, slot_at(rel), 4 + n, sib_rel(rel), (sibling, t)))

    def q_waits(h):
        for rel in (1, 3, 5, 7):
            q_wait(h, rel)

    def attend(h, slot, num_at, den_at):
        group = group_ref[p * 8 + slot]
        for j in range(8):
            block = kvb[h][owner_ref[group, j]]
            kscr[j * SL : (j + 1) * SL, :] = block[:, :HD]
            vscr[j * SL : (j + 1) * SL, :HD] = block[:, HD:]
        scores = lax.dot_general(qb[h][slot], kscr[...], contract, preferred_element_type=F32)
        both = jnp.dot(weigh(scores).astype(BF), vscr[...], preferred_element_type=F32)
        num_at[...] = both[:, :HD].astype(BF)
        for g in range(4):
            den = both[g * HD : (g + 1) * HD, HD:]
            den_at[g : g + 1, :] = jnp.sum(jnp.where(eye, den, 0.0), axis=0, keepdims=True)

    def back_num(h, rel):
        slot = slot_at(rel)
        return copy_to(ns[h].at[slot], nr[h].at[s], rs.at[h, rel], rr.at[h, rel], row_dev(slot))

    def back_den(h, rel):
        slot = slot_at(rel)
        return copy_to(ds[h].at[slot], dr[h].at[s], es.at[h, rel], er.at[h, rel], row_dev(slot))

    def attend_loop(h, first, last):
        @pl.loop(first, last)
        def _(rel):
            slot = slot_at(rel)
            attend(h, slot, ns[h].at[slot], ds[h].at[slot])
            back_num(h, rel).start()
            back_den(h, rel).start()

    def combine(h):
        for rel in range(1, 8):
            src = slot_at(8 - rel)
            copy_to(nr[h].at[src], nr[h].at[src], rs.at[h, rel], rr.at[h, rel], row_dev(s)).wait_recv()
            copy_to(dr[h].at[src], dr[h].at[src], es.at[h, rel], er.at[h, rel], row_dev(s)).wait_recv()
        den_rows = dr[h][0]
        for i in range(1, 8):
            den_rows = den_rows + dr[h][i]
        for g in range(4):
            at = slice(g * HD, (g + 1) * HD)
            spread = jnp.where(eye, jnp.broadcast_to(den_rows[g : g + 1, :], (HD, HD)), 0.0)
            den = jnp.sum(spread, axis=1, keepdims=True) + sden[h, at, :]
            num = snum[h, at, :]
            for i in range(8):
                num = num + nr[h][i, at, :].astype(F32)
            r0 = (g % 2) * HD
            head = 2 * h + g // 2
            rows_live = (lax.broadcasted_iota(jnp.int32, (HD, HD), 0) + r0) < length_ref[me]
            out = jnp.where(rows_live, num / den, 0.0).astype(BF)
            att_ref[r0 : r0 + HD, head * HD : (head + 1) * HD] = out

    q_waits(0)
    attend_loop(0, 1, 3)
    z_step(1, 0)
    attend_loop(0, 3, 6)
    z_step(1, 1)
    attend_loop(0, 6, 8)
    attend(0, s, nr[0].at[s], dr[0].at[s])
    q_waits(1)
    z_step(1, 2)
    attend_loop(1, 1, 8)
    attend(1, s, nr[1].at[s], dr[1].at[s])
    combine(0)
    combine(1)

    for copy in pending:
        copy.wait_send()
    for h in range(2):
        for rel in range(1, 8):
            back_num(h, rel).wait_send()
            back_den(h, rel).wait_send()

    @pl.when(mid)
    def _():
        for h in range(2):
            z_copy(h, 0, "second").wait_send()
            for k in range(3):
                z_copy(h, k, "relay").wait_send()


def body(hidden, norm_gain, w_query, w_key, w_value, prefix_kv, group_of, block_owner, lengths):
    kv = prefix_kv.reshape(512, 2, 2, HD).transpose(2, 0, 1, 3).reshape(2, 512, 2 * HD)
    gain = norm_gain.reshape(1, TP * FEAT)
    full_cos, signed_sin = rope_constants()
    smem = pl.BlockSpec(memory_space=pltpu.SMEM)
    vmem = pl.BlockSpec(memory_space=pltpu.VMEM)
    hbm = pl.BlockSpec(memory_space=pl.ANY)
    dma = pltpu.SemaphoreType.DMA
    pair = lambda shape, dtype: [pltpu.VMEM(shape, dtype)] * 2
    return pl.pallas_call(
        kernel,
        out_shape=(
            jax.ShapeDtypeStruct((ROWS, 512), BF),
            jax.ShapeDtypeStruct((ROWS, 256), BF),
            jax.ShapeDtypeStruct((ROWS, 256), BF),
        ),
        in_specs=[smem] * 3 + [hbm] * 5 + [vmem] * 3,
        out_specs=(vmem, vmem, vmem),
        scratch_shapes=[
            pltpu.VMEM((TP, FEAT, ROWS), BF),
            pltpu.VMEM((TP * FEAT, 1024), BF),
            *pair((32, SL, 256), BF),
            *pair((8, 512, HD), BF),
            *pair((8, 512, HD), BF),
            *pair((8, 512, HD), BF),
            *pair((8, 8, HD), F32),
            *pair((8, 8, HD), F32),
            pltpu.VMEM((ROWS, 1024), F32),
            pltpu.VMEM((TP, 8, ROWS), F32),
            pltpu.VMEM((TP * FEAT, HD), F32),
            pltpu.VMEM((512, HD), BF),
            pltpu.VMEM((512, 2 * HD), BF),
            pltpu.VMEM((2, 512, HD), F32),
            pltpu.VMEM((2, 512, HD), F32),
            dma((3,)), dma((3,)), dma((8,)), dma((8,)), dma((7,)), dma((7,)),
            dma((2, 8)), dma((2, 8)), dma((2, 5)), dma((2, 3)),
            dma((2, 8)), dma((2, 8)), dma((2, 8)), dma((2, 8)), dma((2, 8)), dma((2, 8)),
        ],
        name="prefill",
        compiler_params=pltpu.CompilerParams(
            collective_id=1, has_side_effects=True, vmem_limit_bytes=56 * 2**20
        ),
    )(
        group_of, block_owner, lengths, hidden.T, w_query, w_key, w_value, kv, gain,
        jnp.asarray(full_cos), jnp.asarray(signed_sin),
    )


def solution(mesh):
    in_specs = (
        P("req", "tp"), P(), P(None, "tp"), P(None, "tp"), P(None, "tp"),
        P("req", None, "tp"), P(), P(), P(),
    )
    out_specs = (P("req", "tp"), P("req", "tp"), P("req", "tp"))
    return jax.shard_map(body, mesh=mesh, in_specs=in_specs, out_specs=out_specs, check_vma=False)
```

```python
import functools
import math

import jax
import jax.numpy as jnp
import numpy as np
from jax import lax
from jax.experimental import pallas as pl
from jax.experimental.pallas import tpu as pltpu
from jax.sharding import PartitionSpec as P

MESH = pl.DeviceIdType.MESH
BF = jnp.bfloat16
F32 = jnp.float32
HD = 128
ROWS = 256
PREFIX = 4096
FEAT = 576
TP = 8
SL = 64
LOG2E = 1.4426950408889634


def rope_constants():
    freq = np.exp(np.arange(64, dtype=np.float32) * np.float32(-2.0 * math.log(10000.0) / 128))
    angle = (np.arange(ROWS) + PREFIX).astype(np.float32)[:, None] * freq[None, :]
    cosine, sine = np.cos(angle.astype(np.float64)), np.sin(angle.astype(np.float64))
    full_cos = np.concatenate([cosine, cosine], axis=1).astype(np.float32)
    signed_sin = np.concatenate([-sine, sine], axis=1).astype(np.float32)
    return full_cos, signed_sin


def kernel(
    group_ref, owner_ref, length_ref, hid, wq, wk, wv, kv, gain_ref, cos_ref, sin_ref,
    att_ref, key_ref, val_ref,
    hbuf, wbuf, kraw, kf32, kvs, kvb0, kvb1, qb0, qb1, ns0, ns1, nl0, nl1, ds0, ds1, dl0, dl1,
    acc, sq, gcol, kscr, vscr, snum, sden,
    lsem, wsem, qss, qsr, hs, hr, cs, cr, zs, zr, qs, qr, rs, rr, es, er,
):
    kvb, qb, ns, nl, ds, dl = (kvb0, kvb1), (qb0, qb1), (ns0, ns1), (nl0, nl1), (ds0, ds1), (dl0, dl1)
    me = lax.axis_index("req")
    t = lax.axis_index("tp")
    p, s = me // 8, me % 8
    x, c = s // 2, s % 2
    zh, y = t // 4, t % 4
    inner = (p * (3 - p)) // 2
    mid = inner == 1
    zo = (p + 1 - 2 * (p % 2), 2 - p // 2, 3 - 3 * (p // 2))

    def row_dev(slot):
        return (p * 8 + slot, t)

    def z_dev(z):
        return (z * 8 + s, t)

    def tp_dev(other):
        return (me, other)

    def slot_at(rel):
        return (s + rel) % 8

    def copy_to(src, dst, send, recv, dev):
        return pltpu.make_async_remote_copy(src, dst, send, recv, device_id=dev, device_id_type=MESH)

    sibling = p * 8 + s + 1 - 2 * c
    here, there = zh * 4, (1 - zh) * 4
    yp, ym, yq = (y + 1) % 4, (y + 3) % 4, (y + 2) % 4

    own_hid = pltpu.make_async_copy(hid, hbuf.at[t], lsem.at[0])
    own_hid.start()
    own_kv = pltpu.make_async_copy(kv, kraw, lsem.at[1])
    own_kv.start()
    loads = [
        pltpu.make_async_copy(wq, wbuf.at[:, 0:512], wsem.at[0]),
        pltpu.make_async_copy(wk, wbuf.at[:, 512:768], wsem.at[1]),
        pltpu.make_async_copy(wv, wbuf.at[:, 768:1024], wsem.at[2]),
    ]
    for load in loads:
        load.start()

    barrier = pltpu.get_barrier_semaphore()
    greet = [row_dev(slot_at(rel)) for rel in range(1, 8)]
    greet += [z_dev(zo[0])] + [tp_dev((t + i) % TP) for i in range(1, TP)]
    for dev in greet:
        pl.semaphore_signal(barrier, inc=1, device_id=dev, device_id_type=MESH)

    @pl.when(mid)
    def _():
        pl.semaphore_signal(barrier, inc=1, device_id=z_dev(3 - p), device_id_type=MESH)

    eye = lax.broadcasted_iota(jnp.int32, (HD, HD), 0) == lax.broadcasted_iota(jnp.int32, (HD, HD), 1)
    own_hid.wait()
    features = hbuf[t].astype(F32)
    sq[t] = jnp.broadcast_to(jnp.sum(features * features, axis=0, keepdims=True), (8, ROWS))
    own_kv.wait()
    for h in range(2):
        kf32[...] = kraw[:, :, h * HD : (h + 1) * HD].astype(F32).reshape(1024, HD)
        kvs[h, :, :HD] = kf32[pl.ds(0, 512, stride=2), :].astype(BF)
        kvs[h, :, HD:] = kf32[pl.ds(1, 512, stride=2), :].astype(BF)
    for h in range(2):
        kvb[h][me] = kvs[h, pl.ds(pl.multiple_of(s * SL, SL), SL), :]
    pl.semaphore_wait(barrier, len(greet) + inner)

    pending = []

    def go(copy):
        copy.start()
        pending.append(copy)

    def hid_ref(holder, half):
        if half is None:
            return hbuf.at[holder]
        return hbuf.at[holder, pl.ds(half * (FEAT // 2), FEAT // 2)]

    def hid_copy(i, holder, half, dev):
        ref = hid_ref(holder, half)
        go(copy_to(ref, ref, hs.at[i], hr.at[i], tp_dev(dev)))

    def hid_wait(i, holder, half):
        ref = hid_ref(holder, half)
        copy_to(ref, ref, hs.at[i], hr.at[i], tp_dev(t)).wait_recv()

    def sq_copy(i):
        return copy_to(sq.at[t], sq.at[t], qss.at[i], qsr.at[i], tp_dev((t + i) % TP))

    def sq_wait(i):
        ref = sq.at[(t + TP - i) % TP]
        copy_to(ref, ref, qss.at[i], qsr.at[i], tp_dev(t)).wait_recv()

    def scatter(h, rel):
        slot = slot_at(rel)
        src = kvs.at[h, pl.ds(pl.multiple_of(slot * SL, SL), SL)]
        return copy_to(src, kvb[h].at[me], cs.at[h, rel], cr.at[h, rel], row_dev(slot))

    def scatter_wait(h, rel):
        ref = kvb[h].at[p * 8 + slot_at(8 - rel)]
        copy_to(ref, ref, cs.at[h, rel], cr.at[h, rel], row_dev(s)).wait_recv()

    def z_rows(h, z):
        return kvb[h].at[pl.ds(pl.multiple_of(z * 8, 8), 8)]

    def z_copy(h, k, which):
        if which == "first":
            ref, target, sem, at = z_rows(h, p), zo[0], 0, 0
        elif which == "second":
            ref, target, sem, at = z_rows(h, p), 3 - p, 1, 1
        else:
            ref, target, sem = z_rows(h, zo[k]), (3 - p if k == 0 else 3 * p - 3), 2 + k
            at = (2, 1, 2)[k]
        return copy_to(ref, ref, zs.at[h, sem], zr.at[h, at], z_dev(target))

    def z_own(h):
        go(z_copy(h, 0, "first"))

        @pl.when(mid)
        def _():
            z_copy(h, 0, "second").start()

    def z_step(h, k):
        ref = z_rows(h, zo[k])
        copy_to(ref, ref, zs.at[h, 0], zr.at[h, k], z_dev(p)).wait_recv()

        @pl.when(mid)
        def _():
            z_copy(h, k, "relay").start()

    def project(holder, row_scale):
        at = pl.ds(pl.multiple_of(holder * FEAT, FEAT), FEAT)
        gain = gcol[at, :]
        normed = hbuf[holder].astype(F32) * row_scale * jnp.concatenate([gain, gain], axis=1)
        acc[...] += lax.dot_general(
            normed.astype(BF), wbuf[at, :], (((0,), (0,)), ((), ())), preferred_element_type=F32
        )

    for i in range(1, TP):
        go(sq_copy(i))
    hid_copy(0, t, 0, there + y)
    hid_copy(1, t, 1, there + y)
    hid_copy(2, t, None, here + yp)
    hid_copy(3, t, None, here + ym)
    for h in range(2):
        for rel in range(1, 8):
            go(scatter(h, rel))

    acc[...] = jnp.zeros_like(acc)
    vscr[...] = jnp.ones_like(vscr)
    for i in range(TP * FEAT // HD):
        at = slice(i * HD, (i + 1) * HD)
        spread = jnp.where(eye, jnp.broadcast_to(gain_ref[:, at], (HD, HD)), 0.0)
        gcol[at, :] = jnp.broadcast_to(jnp.sum(spread, axis=1, keepdims=True), (HD, HD))

    hid_wait(2, here + ym, None)
    hid_copy(4, here + ym, 0, here + yp)
    hid_wait(3, here + yp, None)
    hid_copy(5, here + yp, 1, here + ym)
    for h in range(2):
        for rel in range(1, 8):
            scatter_wait(h, rel)
    hid_wait(0, there + y, 0)
    hid_copy(6, there + y, 0, here + yp)
    hid_copy(7, there + y, 0, here + ym)
    z_own(0)
    for i in range(1, TP):
        sq_wait(i)
    total = sq[0]
    for i in range(1, TP):
        total = total + sq[i]
    row_scale = lax.rsqrt(total[0:1, :] / (TP * FEAT) + 1e-6)
    for load in loads:
        load.wait()
    project(t, row_scale)
    hid_wait(1, there + y, 1)
    hid_copy(8, there + y, 1, here + yp)
    hid_copy(9, there + y, 1, here + ym)
    hid_wait(6, there + ym, 0)
    hid_copy(10, there + ym, 0, here + yp)
    project(here + ym, row_scale)
    project(here + yp, row_scale)
    hid_wait(9, there + yp, 1)
    hid_copy(11, there + yp, 1, here + ym)
    z_step(0, 0)
    project(there + y, row_scale)
    hid_wait(4, here + yq, 0)
    hid_wait(5, here + yq, 1)
    project(here + yq, row_scale)
    hid_wait(8, there + ym, 1)
    project(there + ym, row_scale)
    hid_wait(7, there + yp, 0)
    project(there + yp, row_scale)
    hid_wait(10, there + yq, 0)
    hid_wait(11, there + yq, 1)
    z_step(0, 1)
    z_own(1)
    project(there + yq, row_scale)

    cosine, sine = cos_ref[...], sin_ref[...]
    live = lax.broadcasted_iota(jnp.int32, (ROWS, HD), 0) < length_ref[me]

    def rotated(at):
        v = acc[:, at : at + HD]
        return v * cosine + pltpu.roll(v, 64, 1) * sine

    def q_copy(h, slot, sem, rel, dev):
        ref = qb[h].at[slot]
        return copy_to(ref, ref, qs.at[h, sem], qr.at[h, rel], dev)

    def q_wait(h, rel):
        ref = qb[h].at[slot_at(rel)]
        copy_to(ref, ref, qs.at[h, 0], qr.at[h, rel], row_dev(s)).wait_recv()

    def sib_rel(rel):
        return (rel + 2 * c + 7) % 8

    def weigh(scores):
        return jnp.exp2(jnp.tanh(scores * (1.0 / 50.0)) * (50.0 * LOG2E))

    contract = (((1,), (1,)), ((), ()))
    for h in range(2):
        for g in range(2):
            q = (rotated((2 * h + g) * HD) * (1.0 / 12.0)).astype(BF)
            qb[h][s, g * ROWS : (g + 1) * ROWS, :] = q
    for h in range(2):
        key_ref[:, h * HD : (h + 1) * HD] = jnp.where(live, rotated(512 + h * HD), 0.0).astype(BF)
        v = acc[:, 768 + h * HD : 768 + (h + 1) * HD]
        val_ref[:, h * HD : (h + 1) * HD] = jnp.where(live, v, 0.0).astype(BF)
        for n, rel in enumerate((2, 6, 4)):
            go(q_copy(h, s, n, 8 - rel, row_dev(slot_at(rel))))
        go(q_copy(h, s, 3, sib_rel(0), (sibling, t)))
    z_step(0, 2)

    row_id = lax.broadcasted_iota(jnp.int32, (2 * ROWS, ROWS), 0) % ROWS
    col_id = lax.broadcasted_iota(jnp.int32, (2 * ROWS, ROWS), 1)
    causal = row_id >= col_id
    ones = jnp.ones((ROWS, HD), BF)
    for h in range(2):
        scores = lax.dot_general(
            qb[h][s], key_ref[:, h * HD : (h + 1) * HD], contract, preferred_element_type=F32
        )
        w = jnp.where(causal, weigh(scores), 0.0).astype(BF)
        values = jnp.concatenate([val_ref[:, h * HD : (h + 1) * HD], ones], axis=1)
        both = jnp.dot(w, values, preferred_element_type=F32)
        snum[h] = both[:, :HD]
        sden[h] = both[:, HD:]

    def q_forward(h):
        for n, rel in enumerate((2, 6, 4)):
            q_wait(h, rel)
            go(q_copy(h, slot_at(rel), 4 + n, sib_rel(rel), (sibling, t)))

    def q_rest(h):
        for rel in (1, 3, 5, 7):
            q_wait(h, rel)

    def num_copy(h, i, dev):
        return copy_to(ns[h].at[i], nl[h].at[i], rs.at[h, i], rr.at[h, i], dev)

    def den_copy(h, i, dev):
        return copy_to(ds[h].at[i], dl[h].at[i], es.at[h, i], er.at[h, i], dev)

    def land_wait(h, i):
        num_copy(h, i, row_dev(s)).wait_recv()
        den_copy(h, i, row_dev(s)).wait_recv()

    def attend_loop(h, first, last):
        @pl.loop(first, last)
        def _(i):
            dx = (i + 1) % 4
            core = (1 - c) + (i // 4) * (2 * c - 1)
            slot = ((x + dx) % 4) * 2 + core
            group = group_ref[p * 8 + slot]
            for j in range(8):
                block = kvb[h][owner_ref[group, j]]
                kscr[j * SL : (j + 1) * SL, :] = block[:, :HD]
                vscr[j * SL : (j + 1) * SL, :HD] = block[:, HD:]
            scores = lax.dot_general(qb[h][slot], kscr[...], contract, preferred_element_type=F32)
            both = jnp.dot(weigh(scores).astype(BF), vscr[...], preferred_element_type=F32)

            @pl.when(i < 7)
            def _():
                num = both[:, :HD]
                for g in range(4):
                    den = both[g * HD : (g + 1) * HD, HD:]
                    ds[h][i, g : g + 1, :] = jnp.sum(jnp.where(eye, den, 0.0), axis=0, keepdims=True)

                @pl.when(i < 4)
                def _():
                    ns[h][i] = num.astype(BF)
                    num_copy(h, i, (sibling, t)).start()
                    den_copy(h, i, (sibling, t)).start()

                @pl.when(i >= 4)
                def _():
                    land_wait(h, i - 4)
                    ns[h][i] = (num + nl[h][i - 4].astype(F32)).astype(BF)
                    ds[h][i] = ds[h][i] + dl[h][i - 4]
                    num_copy(h, i, row_dev(slot)).start()
                    den_copy(h, i, row_dev(slot)).start()

            @pl.when(i == 7)
            def _():
                snum[h] += both[:, :HD]
                sden[h] += both[:, HD:]

    def combine(h):
        for i in range(3, 7):
            land_wait(h, i)
        den_rows = dl[h][3] + dl[h][4] + dl[h][5] + dl[h][6]
        for g in range(4):
            at = slice(g * HD, (g + 1) * HD)
            spread = jnp.where(eye, jnp.broadcast_to(den_rows[g : g + 1, :], (HD, HD)), 0.0)
            den = jnp.sum(spread, axis=1, keepdims=True) + sden[h, at, :]
            num = snum[h, at, :]
            for i in range(3, 7):
                num = num + nl[h][i, at, :].astype(F32)
            r0 = (g % 2) * HD
            head = 2 * h + g // 2
            rows_live = (lax.broadcasted_iota(jnp.int32, (HD, HD), 0) + r0) < length_ref[me]
            out = jnp.where(rows_live, num / den, 0.0).astype(BF)
            att_ref[r0 : r0 + HD, head * HD : (head + 1) * HD] = out

    q_forward(0)
    q_rest(0)
    attend_loop(0, 0, 3)
    q_forward(1)
    z_step(1, 0)
    attend_loop(0, 3, 8)
    z_step(1, 1)
    q_rest(1)
    combine(0)
    z_step(1, 2)
    attend_loop(1, 0, 8)
    combine(1)

    for copy in pending:
        copy.wait_send()
    for h in range(2):
        for i in range(7):
            num_copy(h, i, row_dev(s)).wait_send()
            den_copy(h, i, row_dev(s)).wait_send()

    @pl.when(mid)
    def _():
        for h in range(2):
            z_copy(h, 0, "second").wait_send()
            for k in range(3):
                z_copy(h, k, "relay").wait_send()


def finish(att, key, val, att_out, key_out, val_out):
    att_out[...] = att[...]
    key_out[...] = key[...]
    val_out[...] = val[...]


def body(hidden, norm_gain, w_query, w_key, w_value, prefix_kv, group_of, block_owner, lengths):
    gain = norm_gain.reshape(1, TP * FEAT)
    full_cos, signed_sin = rope_constants()
    smem = pl.BlockSpec(memory_space=pltpu.SMEM)
    vmem = pl.BlockSpec(memory_space=pltpu.VMEM)
    hbm = pl.BlockSpec(memory_space=pl.ANY)
    dma = pltpu.SemaphoreType.DMA
    pair = lambda shape, dtype: [pltpu.VMEM(shape, dtype)] * 2
    shapes = tuple(jax.ShapeDtypeStruct((ROWS, n), BF) for n in (512, 256, 256))
    results = pl.pallas_call(
        kernel,
        out_shape=shapes,
        in_specs=[smem] * 3 + [hbm] * 5 + [vmem] * 3,
        out_specs=(vmem, vmem, vmem),
        scratch_shapes=[
            pltpu.VMEM((TP, FEAT, ROWS), BF),
            pltpu.VMEM((TP * FEAT, 1024), BF),
            pltpu.VMEM((512, 2, 256), BF),
            pltpu.VMEM((1024, HD), F32),
            pltpu.VMEM((2, 512, 256), BF),
            *pair((32, SL, 256), BF),
            *pair((8, 512, HD), BF),
            *pair((8, 512, HD), BF),
            *pair((8, 512, HD), BF),
            *pair((8, 8, HD), F32),
            *pair((8, 8, HD), F32),
            pltpu.VMEM((ROWS, 1024), F32),
            pltpu.VMEM((TP, 8, ROWS), F32),
            pltpu.VMEM((TP * FEAT, HD), F32),
            pltpu.VMEM((512, HD), BF),
            pltpu.VMEM((512, 2 * HD), BF),
            pltpu.VMEM((2, 512, HD), F32),
            pltpu.VMEM((2, 512, HD), F32),
            dma((2,)), dma((3,)), dma((8,)), dma((8,)), dma((12,)), dma((12,)),
            dma((2, 8)), dma((2, 8)), dma((2, 5)), dma((2, 3)),
            dma((2, 8)), dma((2, 8)), dma((2, 8)), dma((2, 8)), dma((2, 8)), dma((2, 8)),
        ],
        name="prefill",
        compiler_params=pltpu.CompilerParams(
            collective_id=1, has_side_effects=True, vmem_limit_bytes=56 * 2**20
        ),
    )(
        group_of, block_owner, lengths, hidden.T, w_query, w_key, w_value, prefix_kv, gain,
        jnp.asarray(full_cos), jnp.asarray(signed_sin),
    )
    return pl.pallas_call(
        finish, out_shape=shapes, in_specs=[vmem] * 3, out_specs=(vmem, vmem, vmem), name="finish"
    )(*results)


def solution(mesh):
    in_specs = (
        P("req", "tp"), P(), P(None, "tp"), P(None, "tp"), P(None, "tp"),
        P("req", None, "tp"), P(), P(), P(),
    )
    out_specs = (P("req", "tp"), P("req", "tp"), P("req", "tp"))
    return jax.shard_map(body, mesh=mesh, in_specs=in_specs, out_specs=out_specs, check_vma=False)
```

```python
import functools
import math

import jax
import jax.numpy as jnp
import numpy as np
from jax import lax
from jax.experimental import pallas as pl
from jax.experimental.pallas import tpu as pltpu
from jax.sharding import PartitionSpec as P

MESH = pl.DeviceIdType.MESH
BF = jnp.bfloat16
F32 = jnp.float32
HD = 128
ROWS = 256
PREFIX = 4096
FEAT = 576
TP = 8
SL = 64
LOG2E = 1.4426950408889634


def rope_constants():
    freq = np.exp(np.arange(64, dtype=np.float32) * np.float32(-2.0 * math.log(10000.0) / 128))
    angle = (np.arange(ROWS) + PREFIX).astype(np.float32)[:, None] * freq[None, :]
    cosine, sine = np.cos(angle.astype(np.float64)), np.sin(angle.astype(np.float64))
    full_cos = np.concatenate([cosine, cosine], axis=1).astype(np.float32)
    signed_sin = np.concatenate([-sine, sine], axis=1).astype(np.float32)
    return full_cos, signed_sin


def kernel(
    group_ref, owner_ref, length_ref, hid, wq, wk, wv, kv, gain_ref, cos_ref, sin_ref,
    att_ref, key_ref, val_ref,
    hbuf, wbuf, kraw, kf32, kvs, kvb0, kvb1, qb0, qb1, ns0, ns1, nl0, nl1, ds0, ds1, dl0, dl1,
    acc, sq, gcol, kscr, vscr, snum, sden,
    lsem, wsem, qss, qsr, hs, hr, cs, cr, zs, zr, qs, qr, rs, rr, es, er,
):
    kvb, qb, ns, nl, ds, dl = (kvb0, kvb1), (qb0, qb1), (ns0, ns1), (nl0, nl1), (ds0, ds1), (dl0, dl1)
    me = lax.axis_index("req")
    t = lax.axis_index("tp")
    p, s = me // 8, me % 8
    x, c = s // 2, s % 2
    zh, y = t // 4, t % 4
    inner = (p * (3 - p)) // 2
    mid = inner == 1
    zo = (p + 1 - 2 * (p % 2), 2 - p // 2, 3 - 3 * (p // 2))

    def row_dev(slot):
        return (p * 8 + slot, t)

    def z_dev(z):
        return (z * 8 + s, t)

    def tp_dev(other):
        return (me, other)

    def slot_at(rel):
        return (s + rel) % 8

    def copy_to(src, dst, send, recv, dev):
        return pltpu.make_async_remote_copy(src, dst, send, recv, device_id=dev, device_id_type=MESH)

    sibling = p * 8 + s + 1 - 2 * c
    here, there = zh * 4, (1 - zh) * 4
    yp, ym, yq = (y + 1) % 4, (y + 3) % 4, (y + 2) % 4

    own_hid = pltpu.make_async_copy(hid, hbuf.at[t], lsem.at[0])
    own_hid.start()
    own_kv = pltpu.make_async_copy(kv, kraw, lsem.at[1])
    own_kv.start()
    loads = [
        pltpu.make_async_copy(wq, wbuf.at[:, 0:512], wsem.at[0]),
        pltpu.make_async_copy(wk, wbuf.at[:, 512:768], wsem.at[1]),
        pltpu.make_async_copy(wv, wbuf.at[:, 768:1024], wsem.at[2]),
    ]
    for load in loads:
        load.start()

    barrier = pltpu.get_barrier_semaphore()
    greet = [row_dev(slot_at(rel)) for rel in range(1, 8)]
    greet += [z_dev(zo[0])] + [tp_dev((t + i) % TP) for i in range(1, TP)]
    for dev in greet:
        pl.semaphore_signal(barrier, inc=1, device_id=dev, device_id_type=MESH)

    @pl.when(mid)
    def _():
        pl.semaphore_signal(barrier, inc=1, device_id=z_dev(3 - p), device_id_type=MESH)

    eye = lax.broadcasted_iota(jnp.int32, (HD, HD), 0) == lax.broadcasted_iota(jnp.int32, (HD, HD), 1)
    pl.semaphore_wait(barrier, len(greet) + inner)

    pending = []

    def go(copy):
        copy.start()
        pending.append(copy)

    def hid_ref(holder, half):
        if half is None:
            return hbuf.at[holder]
        return hbuf.at[holder, pl.ds(half * (FEAT // 2), FEAT // 2)]

    def hid_copy(i, holder, half, dev):
        ref = hid_ref(holder, half)
        go(copy_to(ref, ref, hs.at[i], hr.at[i], tp_dev(dev)))

    def hid_wait(i, holder, half):
        ref = hid_ref(holder, half)
        copy_to(ref, ref, hs.at[i], hr.at[i], tp_dev(t)).wait_recv()

    def sq_copy(i):
        return copy_to(sq.at[t], sq.at[t], qss.at[i], qsr.at[i], tp_dev((t + i) % TP))

    def sq_wait(i):
        ref = sq.at[(t + TP - i) % TP]
        copy_to(ref, ref, qss.at[i], qsr.at[i], tp_dev(t)).wait_recv()

    def scatter(h, rel):
        slot = slot_at(rel)
        src = kvs.at[h, pl.ds(pl.multiple_of(slot * SL, SL), SL)]
        return copy_to(src, kvb[h].at[me], cs.at[h, rel], cr.at[h, rel], row_dev(slot))

    def scatter_wait(h, rel):
        ref = kvb[h].at[p * 8 + slot_at(8 - rel)]
        copy_to(ref, ref, cs.at[h, rel], cr.at[h, rel], row_dev(s)).wait_recv()

    def z_rows(h, z):
        return kvb[h].at[pl.ds(pl.multiple_of(z * 8, 8), 8)]

    def z_copy(h, k, which):
        if which == "first":
            ref, target, sem, at = z_rows(h, p), zo[0], 0, 0
        elif which == "second":
            ref, target, sem, at = z_rows(h, p), 3 - p, 1, 1
        else:
            ref, target, sem = z_rows(h, zo[k]), (3 - p if k == 0 else 3 * p - 3), 2 + k
            at = (2, 1, 2)[k]
        return copy_to(ref, ref, zs.at[h, sem], zr.at[h, at], z_dev(target))

    def z_own(h):
        go(z_copy(h, 0, "first"))

        @pl.when(mid)
        def _():
            z_copy(h, 0, "second").start()

    def z_wait(h, k):
        ref = z_rows(h, zo[k])
        copy_to(ref, ref, zs.at[h, 0], zr.at[h, k], z_dev(p)).wait_recv()

    def z_relay(h, *ks):
        @pl.when(mid)
        def _():
            for k in ks:
                z_wait(h, k)
                z_copy(h, k, "relay").start()

    def z_take(h):
        @pl.when(inner == 0)
        def _():
            for k in range(3):
                z_wait(h, k)

    def project(holder, row_scale):
        at = pl.ds(pl.multiple_of(holder * FEAT, FEAT), FEAT)
        gain = gcol[at, :]
        normed = hbuf[holder].astype(F32) * row_scale * jnp.concatenate([gain, gain], axis=1)
        acc[...] += lax.dot_general(
            normed.astype(BF), wbuf[at, :], (((0,), (0,)), ((), ())), preferred_element_type=F32
        )

    for half in range(2):
        src = hid.at[pl.ds(half * (FEAT // 2), FEAT // 2)]
        go(copy_to(src, hid_ref(t, half), hs.at[half], hr.at[half], tp_dev(there + y)))
    go(copy_to(hid, hid_ref(t, None), hs.at[2], hr.at[2], tp_dev(here + yp)))
    go(copy_to(hid, hid_ref(t, None), hs.at[3], hr.at[3], tp_dev(here + ym)))
    own_hid.wait()
    features = hbuf[t].astype(F32)
    sq[t] = jnp.broadcast_to(jnp.sum(features * features, axis=0, keepdims=True), (8, ROWS))
    own_kv.wait()
    for h in range(2):
        kf32[...] = kraw[:, :, h * HD : (h + 1) * HD].astype(F32).reshape(1024, HD)
        kvs[h, :, :HD] = kf32[pl.ds(0, 512, stride=2), :].astype(BF)
        kvs[h, :, HD:] = kf32[pl.ds(1, 512, stride=2), :].astype(BF)
    for h in range(2):
        kvb[h][me] = kvs[h, pl.ds(pl.multiple_of(s * SL, SL), SL), :]
    for i in range(1, TP):
        go(sq_copy(i))
    for h in range(2):
        for rel in range(1, 8):
            go(scatter(h, rel))

    acc[...] = jnp.zeros_like(acc)
    vscr[...] = jnp.ones_like(vscr)
    for i in range(TP * FEAT // HD):
        at = slice(i * HD, (i + 1) * HD)
        spread = jnp.where(eye, jnp.broadcast_to(gain_ref[at].reshape(1, HD), (HD, HD)), 0.0)
        gcol[at, :] = jnp.broadcast_to(jnp.sum(spread, axis=1, keepdims=True), (HD, HD))

    def scatter_waits(h):
        for rel in range(1, 8):
            scatter_wait(h, rel)

    scatter_waits(0)
    z_own(0)
    hid_wait(2, here + ym, None)
    hid_copy(4, here + ym, 0, here + yp)
    hid_wait(3, here + yp, None)
    hid_copy(5, here + yp, 1, here + ym)
    hid_wait(0, there + y, 0)
    hid_copy(6, there + y, 0, here + yp)
    hid_copy(7, there + y, 0, here + ym)
    scatter_waits(1)
    z_own(1)
    for i in range(1, TP):
        sq_wait(i)
    total = sq[0]
    for i in range(1, TP):
        total = total + sq[i]
    row_scale = lax.rsqrt(total[0:1, :] / (TP * FEAT) + 1e-6)
    for load in loads:
        load.wait()
    project(t, row_scale)
    project(here + ym, row_scale)
    hid_wait(6, there + ym, 0)
    hid_copy(10, there + ym, 0, here + yp)
    project(here + yp, row_scale)
    hid_wait(1, there + y, 1)
    hid_copy(8, there + y, 1, here + yp)
    hid_copy(9, there + y, 1, here + ym)
    z_relay(0, 0, 1)
    hid_wait(4, here + yq, 0)
    hid_wait(5, here + yq, 1)
    project(here + yq, row_scale)
    project(there + y, row_scale)
    hid_wait(9, there + yp, 1)
    hid_copy(11, there + yp, 1, here + ym)
    hid_wait(8, there + ym, 1)
    project(there + ym, row_scale)
    hid_wait(7, there + yp, 0)
    project(there + yp, row_scale)
    hid_wait(10, there + yq, 0)
    hid_wait(11, there + yq, 1)
    project(there + yq, row_scale)

    cosine, sine = cos_ref[...], sin_ref[...]
    live = lax.broadcasted_iota(jnp.int32, (ROWS, HD), 0) < length_ref[me]

    def rotated(at):
        v = acc[:, at : at + HD]
        return v * cosine + pltpu.roll(v, 64, 1) * sine

    def q_copy(h, slot, sem, rel, dev):
        ref = qb[h].at[slot]
        return copy_to(ref, ref, qs.at[h, sem], qr.at[h, rel], dev)

    def q_wait(h, rel):
        ref = qb[h].at[slot_at(rel)]
        copy_to(ref, ref, qs.at[h, 0], qr.at[h, rel], row_dev(s)).wait_recv()

    def sib_rel(rel):
        return (rel + 2 * c + 7) % 8

    def weigh(scores):
        return jnp.exp2(jnp.tanh(scores * (1.0 / 50.0)) * (50.0 * LOG2E))

    contract = (((1,), (1,)), ((), ()))
    for h in range(2):
        for g in range(2):
            q = (rotated((2 * h + g) * HD) * (1.0 / 12.0)).astype(BF)
            qb[h][s, g * ROWS : (g + 1) * ROWS, :] = q
    for h in range(2):
        key_ref[:, h * HD : (h + 1) * HD] = jnp.where(live, rotated(512 + h * HD), 0.0).astype(BF)
        v = acc[:, 768 + h * HD : 768 + (h + 1) * HD]
        val_ref[:, h * HD : (h + 1) * HD] = jnp.where(live, v, 0.0).astype(BF)
        for n, rel in enumerate((2, 6, 4)):
            go(q_copy(h, s, n, 8 - rel, row_dev(slot_at(rel))))
        go(q_copy(h, s, 3, sib_rel(0), (sibling, t)))
    row_id = lax.broadcasted_iota(jnp.int32, (2 * ROWS, ROWS), 0) % ROWS
    col_id = lax.broadcasted_iota(jnp.int32, (2 * ROWS, ROWS), 1)
    causal = row_id >= col_id
    ones = jnp.ones((ROWS, HD), BF)
    for h in range(2):
        scores = lax.dot_general(
            qb[h][s], key_ref[:, h * HD : (h + 1) * HD], contract, preferred_element_type=F32
        )
        w = jnp.where(causal, weigh(scores), 0.0).astype(BF)
        values = jnp.concatenate([val_ref[:, h * HD : (h + 1) * HD], ones], axis=1)
        both = jnp.dot(w, values, preferred_element_type=F32)
        snum[h] = both[:, :HD]
        sden[h] = both[:, HD:]

    def q_forward(h):
        for n, rel in enumerate((2, 6, 4)):
            q_wait(h, rel)
            go(q_copy(h, slot_at(rel), 4 + n, sib_rel(rel), (sibling, t)))

    def q_rest(h):
        for rel in (1, 3, 5, 7):
            q_wait(h, rel)

    def num_copy(h, i, dev):
        return copy_to(ns[h].at[i], nl[h].at[i], rs.at[h, i], rr.at[h, i], dev)

    def den_copy(h, i, dev):
        return copy_to(ds[h].at[i], dl[h].at[i], es.at[h, i], er.at[h, i], dev)

    def land_wait(h, i):
        num_copy(h, i, row_dev(s)).wait_recv()
        den_copy(h, i, row_dev(s)).wait_recv()

    def attend_loop(h, first, last):
        @pl.loop(first, last)
        def _(i):
            dx = (i + 1) % 4
            core = (1 - c) + (i // 4) * (2 * c - 1)
            slot = ((x + dx) % 4) * 2 + core
            group = group_ref[p * 8 + slot]
            for j in range(8):
                block = kvb[h][owner_ref[group, j]]
                kscr[j * SL : (j + 1) * SL, :] = block[:, :HD]
                vscr[j * SL : (j + 1) * SL, :HD] = block[:, HD:]
            scores = lax.dot_general(qb[h][slot], kscr[...], contract, preferred_element_type=F32)
            both = jnp.dot(weigh(scores).astype(BF), vscr[...], preferred_element_type=F32)

            @pl.when(i < 7)
            def _():
                num = both[:, :HD]
                for g in range(4):
                    den = both[g * HD : (g + 1) * HD, HD:]
                    ds[h][i, g : g + 1, :] = jnp.sum(jnp.where(eye, den, 0.0), axis=0, keepdims=True)

                @pl.when(i < 4)
                def _():
                    ns[h][i] = num.astype(BF)
                    num_copy(h, i, (sibling, t)).start()
                    den_copy(h, i, (sibling, t)).start()

                @pl.when(i >= 4)
                def _():
                    land_wait(h, i - 4)
                    ns[h][i] = (num + nl[h][i - 4].astype(F32)).astype(BF)
                    ds[h][i] = ds[h][i] + dl[h][i - 4]
                    num_copy(h, i, row_dev(slot)).start()
                    den_copy(h, i, row_dev(slot)).start()

            @pl.when(i == 7)
            def _():
                snum[h] += both[:, :HD]
                sden[h] += both[:, HD:]

    def combine(h):
        for i in range(3, 7):
            land_wait(h, i)
        den_rows = dl[h][3] + dl[h][4] + dl[h][5] + dl[h][6]
        for g in range(4):
            at = slice(g * HD, (g + 1) * HD)
            spread = jnp.where(eye, jnp.broadcast_to(den_rows[g : g + 1, :], (HD, HD)), 0.0)
            den = jnp.sum(spread, axis=1, keepdims=True) + sden[h, at, :]
            num = snum[h, at, :]
            for i in range(3, 7):
                num = num + nl[h][i, at, :].astype(F32)
            r0 = (g % 2) * HD
            head = 2 * h + g // 2
            rows_live = (lax.broadcasted_iota(jnp.int32, (HD, HD), 0) + r0) < length_ref[me]
            out = jnp.where(rows_live, num / den, 0.0).astype(BF)
            att_ref[r0 : r0 + HD, head * HD : (head + 1) * HD] = out

    z_relay(0, 2)
    z_relay(1, 0, 1)
    q_forward(0)
    q_rest(0)
    z_take(0)
    attend_loop(0, 0, 4)
    q_forward(1)
    z_relay(1, 2)
    attend_loop(0, 4, 8)
    q_rest(1)
    combine(0)
    z_take(1)
    attend_loop(1, 0, 8)
    combine(1)

    for copy in pending:
        copy.wait_send()
    for h in range(2):
        for i in range(7):
            num_copy(h, i, row_dev(s)).wait_send()
            den_copy(h, i, row_dev(s)).wait_send()

    @pl.when(mid)
    def _():
        for h in range(2):
            z_copy(h, 0, "second").wait_send()
            for k in range(3):
                z_copy(h, k, "relay").wait_send()


def finish(att, key, val, att_out, key_out, val_out):
    att_out[...] = att[...]
    key_out[...] = key[...]
    val_out[...] = val[...]


def body(hidden, norm_gain, w_query, w_key, w_value, prefix_kv, group_of, block_owner, lengths):
    full_cos, signed_sin = rope_constants()
    smem = pl.BlockSpec(memory_space=pltpu.SMEM)
    vmem = pl.BlockSpec(memory_space=pltpu.VMEM)
    hbm = pl.BlockSpec(memory_space=pl.ANY)
    dma = pltpu.SemaphoreType.DMA
    pair = lambda shape, dtype: [pltpu.VMEM(shape, dtype)] * 2
    shapes = tuple(jax.ShapeDtypeStruct((ROWS, n), BF) for n in (512, 256, 256))
    results = pl.pallas_call(
        kernel,
        out_shape=shapes,
        in_specs=[smem] * 3 + [hbm] * 5 + [vmem] * 3,
        out_specs=(vmem, vmem, vmem),
        scratch_shapes=[
            pltpu.VMEM((TP, FEAT, ROWS), BF),
            pltpu.VMEM((TP * FEAT, 1024), BF),
            pltpu.VMEM((512, 2, 256), BF),
            pltpu.VMEM((1024, HD), F32),
            pltpu.VMEM((2, 512, 256), BF),
            *pair((32, SL, 256), BF),
            *pair((8, 512, HD), BF),
            *pair((8, 512, HD), BF),
            *pair((8, 512, HD), BF),
            *pair((8, 8, HD), F32),
            *pair((8, 8, HD), F32),
            pltpu.VMEM((ROWS, 1024), F32),
            pltpu.VMEM((TP, 8, ROWS), F32),
            pltpu.VMEM((TP * FEAT, HD), F32),
            pltpu.VMEM((512, HD), BF),
            pltpu.VMEM((512, 2 * HD), BF),
            pltpu.VMEM((2, 512, HD), F32),
            pltpu.VMEM((2, 512, HD), F32),
            dma((2,)), dma((3,)), dma((8,)), dma((8,)), dma((12,)), dma((12,)),
            dma((2, 8)), dma((2, 8)), dma((2, 5)), dma((2, 3)),
            dma((2, 8)), dma((2, 8)), dma((2, 8)), dma((2, 8)), dma((2, 8)), dma((2, 8)),
        ],
        name="prefill",
        compiler_params=pltpu.CompilerParams(
            collective_id=1, has_side_effects=True, vmem_limit_bytes=56 * 2**20
        ),
    )(
        group_of, block_owner, lengths, hidden.T, w_query, w_key, w_value, prefix_kv, norm_gain,
        jnp.asarray(full_cos), jnp.asarray(signed_sin),
    )
    return pl.pallas_call(
        finish, out_shape=shapes, in_specs=[vmem] * 3, out_specs=(vmem, vmem, vmem), name="finish",
        compiler_params=pltpu.CompilerParams(vmem_limit_bytes=4 * 2**20),
    )(*results)


def solution(mesh):
    in_specs = (
        P("req", "tp"), P(), P(None, "tp"), P(None, "tp"), P(None, "tp"),
        P("req", None, "tp"), P(), P(), P(),
    )
    out_specs = (P("req", "tp"), P("req", "tp"), P("req", "tp"))
    return jax.shard_map(body, mesh=mesh, in_specs=in_specs, out_specs=out_specs, check_vma=False)
```

```python
import functools
import math

import jax
import jax.numpy as jnp
import numpy as np
from jax import lax
from jax.experimental import pallas as pl
from jax.experimental.pallas import tpu as pltpu
from jax.sharding import PartitionSpec as P

MESH = pl.DeviceIdType.MESH
BF = jnp.bfloat16
F32 = jnp.float32
HD = 128
ROWS = 256
PREFIX = 4096
FEAT = 576
TP = 8
SL = 64
LOG2E = 1.4426950408889634


def rope_constants():
    freq = np.exp(np.arange(64, dtype=np.float32) * np.float32(-2.0 * math.log(10000.0) / 128))
    angle = (np.arange(ROWS) + PREFIX).astype(np.float32)[:, None] * freq[None, :]
    cosine, sine = np.cos(angle.astype(np.float64)), np.sin(angle.astype(np.float64))
    full_cos = np.concatenate([cosine, cosine], axis=1).astype(np.float32)
    signed_sin = np.concatenate([-sine, sine], axis=1).astype(np.float32)
    return full_cos, signed_sin


def kernel(
    group_ref, owner_ref, length_ref, hid, wq, wk, wv, kv, gain_ref, cos_ref, sin_ref,
    att_ref, key_ref, val_ref,
    hbuf, wbuf, kraw, kf32, kvs, kvb0, kvb1, qb0, qb1, ns0, ns1, nl0, nl1, ds0, ds1, dl0, dl1,
    acc, sq, gcol, kscr, vscr, snum, sden,
    lsem, wsem, qss, qsr, hs, hr, cs, cr, zs, zr, qs, qr, rs, rr, es, er,
):
    kvb, qb, ns, nl, ds, dl = (kvb0, kvb1), (qb0, qb1), (ns0, ns1), (nl0, nl1), (ds0, ds1), (dl0, dl1)
    me = lax.axis_index("req")
    t = lax.axis_index("tp")
    p, s = me // 8, me % 8
    x, c = s // 2, s % 2
    zh, y = t // 4, t % 4
    inner = (p * (3 - p)) // 2
    mid = inner == 1
    zo = (p + 1 - 2 * (p % 2), 2 - p // 2, 3 - 3 * (p // 2))

    def row_dev(slot):
        return (p * 8 + slot, t)

    def z_dev(z):
        return (z * 8 + s, t)

    def tp_dev(other):
        return (me, other)

    def slot_at(rel):
        return (s + rel) % 8

    def copy_to(src, dst, send, recv, dev):
        return pltpu.make_async_remote_copy(src, dst, send, recv, device_id=dev, device_id_type=MESH)

    sibling = p * 8 + s + 1 - 2 * c
    here, there = zh * 4, (1 - zh) * 4
    yp, ym, yq = (y + 1) % 4, (y + 3) % 4, (y + 2) % 4

    own_hid = pltpu.make_async_copy(hid, hbuf.at[t], lsem.at[0])
    own_hid.start()
    own_kv = pltpu.make_async_copy(kv, kraw, lsem.at[1])
    own_kv.start()
    loads = [
        pltpu.make_async_copy(wq, wbuf.at[:, 0:512], wsem.at[0]),
        pltpu.make_async_copy(wk, wbuf.at[:, 512:768], wsem.at[1]),
        pltpu.make_async_copy(wv, wbuf.at[:, 768:1024], wsem.at[2]),
    ]
    for load in loads:
        load.start()

    barrier = pltpu.get_barrier_semaphore()
    greet = [row_dev(slot_at(rel)) for rel in range(1, 8)]
    greet += [z_dev(zo[0])] + [tp_dev((t + i) % TP) for i in range(1, TP)]
    for dev in greet:
        pl.semaphore_signal(barrier, inc=1, device_id=dev, device_id_type=MESH)

    @pl.when(mid)
    def _():
        pl.semaphore_signal(barrier, inc=1, device_id=z_dev(3 - p), device_id_type=MESH)

    eye = lax.broadcasted_iota(jnp.int32, (HD, HD), 0) == lax.broadcasted_iota(jnp.int32, (HD, HD), 1)
    pl.semaphore_wait(barrier, len(greet) + inner)

    pending = []

    def go(copy):
        copy.start()
        pending.append(copy)

    def hid_ref(holder, half):
        if half is None:
            return hbuf.at[holder]
        return hbuf.at[holder, pl.ds(half * (FEAT // 2), FEAT // 2)]

    def hid_copy(i, holder, half, dev):
        ref = hid_ref(holder, half)
        go(copy_to(ref, ref, hs.at[i], hr.at[i], tp_dev(dev)))

    def hid_wait(i, holder, half):
        ref = hid_ref(holder, half)
        copy_to(ref, ref, hs.at[i], hr.at[i], tp_dev(t)).wait_recv()

    def sq_copy(i):
        return copy_to(sq.at[t], sq.at[t], qss.at[i], qsr.at[i], tp_dev((t + i) % TP))

    def sq_wait(i):
        ref = sq.at[(t + TP - i) % TP]
        copy_to(ref, ref, qss.at[i], qsr.at[i], tp_dev(t)).wait_recv()

    def scatter(h, rel):
        slot = slot_at(rel)
        src = kvs.at[h, pl.ds(pl.multiple_of(slot * SL, SL), SL)]
        return copy_to(src, kvb[h].at[me], cs.at[h, rel], cr.at[h, rel], row_dev(slot))

    def scatter_wait(h, rel):
        ref = kvb[h].at[p * 8 + slot_at(8 - rel)]
        copy_to(ref, ref, cs.at[h, rel], cr.at[h, rel], row_dev(s)).wait_recv()

    def z_rows(h, z):
        return kvb[h].at[pl.ds(pl.multiple_of(z * 8, 8), 8)]

    def z_copy(h, k, which):
        if which == "first":
            ref, target, sem, at = z_rows(h, p), zo[0], 0, 0
        elif which == "second":
            ref, target, sem, at = z_rows(h, p), 3 - p, 1, 1
        else:
            ref, target, sem = z_rows(h, zo[k]), (3 - p if k == 0 else 3 * p - 3), 2 + k
            at = (2, 1, 2)[k]
        return copy_to(ref, ref, zs.at[h, sem], zr.at[h, at], z_dev(target))

    def z_own(h):
        go(z_copy(h, 0, "first"))

        @pl.when(mid)
        def _():
            z_copy(h, 0, "second").start()

    def z_wait(h, k):
        ref = z_rows(h, zo[k])
        copy_to(ref, ref, zs.at[h, 0], zr.at[h, k], z_dev(p)).wait_recv()

    def z_relay(h, *ks):
        @pl.when(mid)
        def _():
            for k in ks:
                z_wait(h, k)
                z_copy(h, k, "relay").start()

    def z_take(h):
        @pl.when(inner == 0)
        def _():
            for k in range(3):
                z_wait(h, k)

    def project(holder, row_scale):
        at = pl.ds(pl.multiple_of(holder * FEAT, FEAT), FEAT)
        gain = gcol[at, :]
        normed = hbuf[holder].astype(F32) * row_scale * jnp.concatenate([gain, gain], axis=1)
        acc[...] += lax.dot_general(
            normed.astype(BF), wbuf[at, :], (((0,), (0,)), ((), ())), preferred_element_type=F32
        )

    for half in range(2):
        src = hid.at[pl.ds(half * (FEAT // 2), FEAT // 2)]
        go(copy_to(src, hid_ref(t, half), hs.at[half], hr.at[half], tp_dev(there + y)))
    go(copy_to(hid, hid_ref(t, None), hs.at[2], hr.at[2], tp_dev(here + yp)))
    go(copy_to(hid, hid_ref(t, None), hs.at[3], hr.at[3], tp_dev(here + ym)))
    own_hid.wait()
    features = hbuf[t].astype(F32)
    sq[t] = jnp.broadcast_to(jnp.sum(features * features, axis=0, keepdims=True), (8, ROWS))
    own_kv.wait()
    for h in range(2):
        kf32[...] = kraw[:, :, h * HD : (h + 1) * HD].astype(F32).reshape(1024, HD)
        kvs[h, :, :HD] = kf32[pl.ds(0, 512, stride=2), :].astype(BF)
        kvs[h, :, HD:] = kf32[pl.ds(1, 512, stride=2), :].astype(BF)
    for h in range(2):
        kvb[h][me] = kvs[h, pl.ds(pl.multiple_of(s * SL, SL), SL), :]
    for i in range(1, TP):
        go(sq_copy(i))
    for h in range(2):
        for rel in range(1, 8):
            go(scatter(h, rel))

    acc[...] = jnp.zeros_like(acc)
    vscr[...] = jnp.ones_like(vscr)
    for i in range(TP * FEAT // HD):
        at = slice(i * HD, (i + 1) * HD)
        spread = jnp.where(eye, jnp.broadcast_to(gain_ref[at].reshape(1, HD), (HD, HD)), 0.0)
        gcol[at, :] = jnp.broadcast_to(jnp.sum(spread, axis=1, keepdims=True), (HD, HD))

    def scatter_waits(h):
        for rel in range(1, 8):
            scatter_wait(h, rel)

    scatter_waits(0)
    z_own(0)
    hid_wait(2, here + ym, None)
    hid_copy(4, here + ym, 0, here + yp)
    hid_wait(3, here + yp, None)
    hid_copy(5, here + yp, 1, here + ym)
    hid_wait(0, there + y, 0)
    hid_copy(6, there + y, 0, here + yp)
    hid_copy(7, there + y, 0, here + ym)
    scatter_waits(1)
    z_own(1)
    for i in range(1, TP):
        sq_wait(i)
    total = sq[0]
    for i in range(1, TP):
        total = total + sq[i]
    row_scale = lax.rsqrt(total[0:1, :] / (TP * FEAT) + 1e-6)
    for load in loads:
        load.wait()
    project(t, row_scale)
    project(here + ym, row_scale)
    hid_wait(6, there + ym, 0)
    hid_copy(10, there + ym, 0, here + yp)
    project(here + yp, row_scale)
    hid_wait(1, there + y, 1)
    hid_copy(8, there + y, 1, here + yp)
    hid_copy(9, there + y, 1, here + ym)
    z_relay(0, 0, 1)
    hid_wait(4, here + yq, 0)
    hid_wait(5, here + yq, 1)
    project(here + yq, row_scale)
    project(there + y, row_scale)
    hid_wait(9, there + yp, 1)
    hid_copy(11, there + yp, 1, here + ym)
    hid_wait(8, there + ym, 1)
    project(there + ym, row_scale)
    hid_wait(7, there + yp, 0)
    project(there + yp, row_scale)
    hid_wait(10, there + yq, 0)
    hid_wait(11, there + yq, 1)
    project(there + yq, row_scale)

    cosine, sine = cos_ref[...], sin_ref[...]
    live = lax.broadcasted_iota(jnp.int32, (ROWS, HD), 0) < length_ref[me]

    def rotated(at):
        v = acc[:, at : at + HD]
        return v * cosine + pltpu.roll(v, 64, 1) * sine

    def q_copy(h, slot, sem, rel, dev):
        ref = qb[h].at[slot]
        return copy_to(ref, ref, qs.at[h, sem], qr.at[h, rel], dev)

    def q_wait(h, rel):
        ref = qb[h].at[slot_at(rel)]
        copy_to(ref, ref, qs.at[h, 0], qr.at[h, rel], row_dev(s)).wait_recv()

    def sib_rel(rel):
        return (rel + 2 * c + 7) % 8

    def weigh(scores):
        return jnp.exp2(jnp.tanh(scores * (1.0 / 50.0)) * (50.0 * LOG2E))

    contract = (((1,), (1,)), ((), ()))
    for h in range(2):
        for g in range(2):
            q = (rotated((2 * h + g) * HD) * (1.0 / 12.0)).astype(BF)
            qb[h][s, g * ROWS : (g + 1) * ROWS, :] = q
    for h in range(2):
        key_ref[:, h * HD : (h + 1) * HD] = jnp.where(live, rotated(512 + h * HD), 0.0).astype(BF)
        v = acc[:, 768 + h * HD : 768 + (h + 1) * HD]
        val_ref[:, h * HD : (h + 1) * HD] = jnp.where(live, v, 0.0).astype(BF)
        for n, rel in enumerate((2, 6, 4)):
            go(q_copy(h, s, n, 8 - rel, row_dev(slot_at(rel))))
        go(q_copy(h, s, 3, sib_rel(0), (sibling, t)))
    row_id = lax.broadcasted_iota(jnp.int32, (2 * ROWS, ROWS), 0) % ROWS
    col_id = lax.broadcasted_iota(jnp.int32, (2 * ROWS, ROWS), 1)
    causal = row_id >= col_id
    ones = jnp.ones((ROWS, HD), BF)
    for h in range(2):
        scores = lax.dot_general(
            qb[h][s], key_ref[:, h * HD : (h + 1) * HD], contract, preferred_element_type=F32
        )
        w = jnp.where(causal, weigh(scores), 0.0).astype(BF)
        values = jnp.concatenate([val_ref[:, h * HD : (h + 1) * HD], ones], axis=1)
        both = jnp.dot(w, values, preferred_element_type=F32)
        snum[h] = both[:, :HD]
        sden[h] = both[:, HD:]

    def q_forward(h):
        for n, rel in enumerate((2, 6, 4)):
            q_wait(h, rel)
            go(q_copy(h, slot_at(rel), 4 + n, sib_rel(rel), (sibling, t)))

    def q_rest(h):
        for rel in (1, 3, 5, 7):
            q_wait(h, rel)

    def num_copy(h, i, dev):
        return copy_to(ns[h].at[i], nl[h].at[i], rs.at[h, i], rr.at[h, i], dev)

    def den_copy(h, i, dev):
        return copy_to(ds[h].at[i], dl[h].at[i], es.at[h, i], er.at[h, i], dev)

    def land_wait(h, i):
        num_copy(h, i, row_dev(s)).wait_recv()
        den_copy(h, i, row_dev(s)).wait_recv()

    def attend_loop(h, first, last):
        @pl.loop(first, last)
        def _(n):
            third, rest = n // 3, n % 3
            shuffled = 1 - rest + (rest // 2) * 3 + 4 * third
            i = (1 - third // 2) * shuffled + (third // 2) * (3 + 4 * rest)
            dx = (i + 1) % 4
            core = (1 - c) + (i // 4) * (2 * c - 1)
            slot = ((x + dx) % 4) * 2 + core
            group = group_ref[p * 8 + slot]
            for j in range(8):
                block = kvb[h][owner_ref[group, j]]
                kscr[j * SL : (j + 1) * SL, :] = block[:, :HD]
                vscr[j * SL : (j + 1) * SL, :HD] = block[:, HD:]
            scores = lax.dot_general(qb[h][slot], kscr[...], contract, preferred_element_type=F32)
            both = jnp.dot(weigh(scores).astype(BF), vscr[...], preferred_element_type=F32)

            @pl.when(i < 7)
            def _():
                num = both[:, :HD]
                for g in range(4):
                    den = both[g * HD : (g + 1) * HD, HD:]
                    ds[h][i, g : g + 1, :] = jnp.sum(jnp.where(eye, den, 0.0), axis=0, keepdims=True)

                @pl.when(i < 4)
                def _():
                    ns[h][i] = num.astype(BF)
                    num_copy(h, i, (sibling, t)).start()
                    den_copy(h, i, (sibling, t)).start()

                @pl.when(i >= 4)
                def _():
                    land_wait(h, i - 4)
                    ns[h][i] = (num + nl[h][i - 4].astype(F32)).astype(BF)
                    ds[h][i] = ds[h][i] + dl[h][i - 4]
                    num_copy(h, i, row_dev(slot)).start()
                    den_copy(h, i, row_dev(slot)).start()

            @pl.when(i == 7)
            def _():
                snum[h] += both[:, :HD]
                sden[h] += both[:, HD:]

    def combine(h):
        for i in range(3, 7):
            land_wait(h, i)
        den_rows = dl[h][3] + dl[h][4] + dl[h][5] + dl[h][6]
        for g in range(4):
            at = slice(g * HD, (g + 1) * HD)
            spread = jnp.where(eye, jnp.broadcast_to(den_rows[g : g + 1, :], (HD, HD)), 0.0)
            den = jnp.sum(spread, axis=1, keepdims=True) + sden[h, at, :]
            num = snum[h, at, :]
            for i in range(3, 7):
                num = num + nl[h][i, at, :].astype(F32)
            r0 = (g % 2) * HD
            head = 2 * h + g // 2
            rows_live = (lax.broadcasted_iota(jnp.int32, (HD, HD), 0) + r0) < length_ref[me]
            out = jnp.where(rows_live, num / den, 0.0).astype(BF)
            att_ref[r0 : r0 + HD, head * HD : (head + 1) * HD] = out

    z_relay(0, 2)
    z_relay(1, 0, 1)
    q_forward(0)
    q_rest(0)
    z_take(0)
    attend_loop(0, 0, 4)
    q_forward(1)
    z_relay(1, 2)
    attend_loop(0, 4, 8)
    q_rest(1)
    combine(0)
    z_take(1)
    attend_loop(1, 0, 8)
    combine(1)

    for copy in pending:
        copy.wait_send()
    for h in range(2):
        for i in range(7):
            num_copy(h, i, row_dev(s)).wait_send()
            den_copy(h, i, row_dev(s)).wait_send()

    @pl.when(mid)
    def _():
        for h in range(2):
            z_copy(h, 0, "second").wait_send()
            for k in range(3):
                z_copy(h, k, "relay").wait_send()


def finish(att, key, val, att_out, key_out, val_out):
    att_out[...] = att[...]
    key_out[...] = key[...]
    val_out[...] = val[...]


def body(hidden, norm_gain, w_query, w_key, w_value, prefix_kv, group_of, block_owner, lengths):
    full_cos, signed_sin = rope_constants()
    smem = pl.BlockSpec(memory_space=pltpu.SMEM)
    vmem = pl.BlockSpec(memory_space=pltpu.VMEM)
    hbm = pl.BlockSpec(memory_space=pl.ANY)
    dma = pltpu.SemaphoreType.DMA
    pair = lambda shape, dtype: [pltpu.VMEM(shape, dtype)] * 2
    shapes = tuple(jax.ShapeDtypeStruct((ROWS, n), BF) for n in (512, 256, 256))
    results = pl.pallas_call(
        kernel,
        out_shape=tuple(pltpu.VMEM((ROWS, n), BF) for n in (512, 256, 256)),
        in_specs=[smem] * 3 + [hbm] * 5 + [vmem] * 3,
        out_specs=(vmem, vmem, vmem),
        scratch_shapes=[
            pltpu.VMEM((TP, FEAT, ROWS), BF),
            pltpu.VMEM((TP * FEAT, 1024), BF),
            pltpu.VMEM((512, 2, 256), BF),
            pltpu.VMEM((1024, HD), F32),
            pltpu.VMEM((2, 512, 256), BF),
            *pair((32, SL, 256), BF),
            *pair((8, 512, HD), BF),
            *pair((8, 512, HD), BF),
            *pair((8, 512, HD), BF),
            *pair((8, 8, HD), F32),
            *pair((8, 8, HD), F32),
            pltpu.VMEM((ROWS, 1024), F32),
            pltpu.VMEM((TP, 8, ROWS), F32),
            pltpu.VMEM((TP * FEAT, HD), F32),
            pltpu.VMEM((512, HD), BF),
            pltpu.VMEM((512, 2 * HD), BF),
            pltpu.VMEM((2, 512, HD), F32),
            pltpu.VMEM((2, 512, HD), F32),
            dma((2,)), dma((3,)), dma((8,)), dma((8,)), dma((12,)), dma((12,)),
            dma((2, 8)), dma((2, 8)), dma((2, 5)), dma((2, 3)),
            dma((2, 8)), dma((2, 8)), dma((2, 8)), dma((2, 8)), dma((2, 8)), dma((2, 8)),
        ],
        name="prefill",
        compiler_params=pltpu.CompilerParams(
            collective_id=1, has_side_effects=True, vmem_limit_bytes=56 * 2**20
        ),
    )(
        group_of, block_owner, lengths, hidden.T, w_query, w_key, w_value, prefix_kv, norm_gain,
        jnp.asarray(full_cos), jnp.asarray(signed_sin),
    )
    return pl.pallas_call(
        finish, out_shape=shapes, in_specs=[vmem] * 3, out_specs=(vmem, vmem, vmem), name="finish",
        compiler_params=pltpu.CompilerParams(vmem_limit_bytes=4 * 2**20),
    )(*results)


def solution(mesh):
    in_specs = (
        P("req", "tp"), P(), P(None, "tp"), P(None, "tp"), P(None, "tp"),
        P("req", None, "tp"), P(), P(), P(),
    )
    out_specs = (P("req", "tp"), P("req", "tp"), P("req", "tp"))
    return jax.shard_map(body, mesh=mesh, in_specs=in_specs, out_specs=out_specs, check_vma=False)
```

```python
import functools
import math

import jax
import jax.numpy as jnp
import numpy as np
from jax import lax
from jax.experimental import pallas as pl
from jax.experimental.pallas import tpu as pltpu
from jax.sharding import PartitionSpec as P

MESH = pl.DeviceIdType.MESH
BF = jnp.bfloat16
F32 = jnp.float32
HD = 128
ROWS = 256
PREFIX = 4096
FEAT = 576
TP = 8
SL = 64
LOG2E = 1.4426950408889634


def rope_constants():
    freq = np.exp(np.arange(64, dtype=np.float32) * np.float32(-2.0 * math.log(10000.0) / 128))
    angle = (np.arange(ROWS) + PREFIX).astype(np.float32)[:, None] * freq[None, :]
    cosine, sine = np.cos(angle.astype(np.float64)), np.sin(angle.astype(np.float64))
    full_cos = np.concatenate([cosine, cosine], axis=1).astype(np.float32)
    signed_sin = np.concatenate([-sine, sine], axis=1).astype(np.float32)
    return full_cos, signed_sin


def kernel(
    group_ref, owner_ref, length_ref, hid, wq, wk, wv, kv, gain_hbm, cos_hbm, sin_hbm,
    att_ref, key_ref, val_ref,
    gain_ref, cos_ref, sin_ref, hbuf, wbuf, kraw, kf32, kvs, kvb0, kvb1, qb0, qb1, ns0, ns1, nl0, nl1, ds0, ds1, dl0, dl1,
    acc, sq, gcol, kscr, vscr, snum, sden,
    lsem, wsem, qss, qsr, hs, hr, cs, cr, zs, zr, qs, qr, rs, rr, es, er,
):
    kvb, qb, ns, nl, ds, dl = (kvb0, kvb1), (qb0, qb1), (ns0, ns1), (nl0, nl1), (ds0, ds1), (dl0, dl1)
    me = lax.axis_index("req")
    t = lax.axis_index("tp")
    p, s = me // 8, me % 8
    x, c = s // 2, s % 2
    zh, y = t // 4, t % 4
    inner = (p * (3 - p)) // 2
    mid = inner == 1
    zo = (p + 1 - 2 * (p % 2), 2 - p // 2, 3 - 3 * (p // 2))

    def row_dev(slot):
        return (p * 8 + slot, t)

    def z_dev(z):
        return (z * 8 + s, t)

    def tp_dev(other):
        return (me, other)

    def slot_at(rel):
        return (s + rel) % 8

    def copy_to(src, dst, send, recv, dev):
        return pltpu.make_async_remote_copy(src, dst, send, recv, device_id=dev, device_id_type=MESH)

    sibling = p * 8 + s + 1 - 2 * c
    here, there = zh * 4, (1 - zh) * 4
    yp, ym, yq = (y + 1) % 4, (y + 3) % 4, (y + 2) % 4

    own_hid = pltpu.make_async_copy(hid, hbuf.at[t], lsem.at[0])
    own_hid.start()
    own_kv = pltpu.make_async_copy(kv, kraw, lsem.at[1])
    own_kv.start()
    tables = [
        pltpu.make_async_copy(gain_hbm, gain_ref, lsem.at[2]),
        pltpu.make_async_copy(cos_hbm, cos_ref, lsem.at[3]),
        pltpu.make_async_copy(sin_hbm, sin_ref, lsem.at[4]),
    ]
    loads = [
        pltpu.make_async_copy(wq, wbuf.at[:, 0:512], wsem.at[0]),
        pltpu.make_async_copy(wk, wbuf.at[:, 512:768], wsem.at[1]),
        pltpu.make_async_copy(wv, wbuf.at[:, 768:1024], wsem.at[2]),
    ]
    for load in tables + loads:
        load.start()

    barrier = pltpu.get_barrier_semaphore()
    greet = [row_dev(slot_at(rel)) for rel in range(1, 8)]
    greet += [z_dev(zo[0])] + [tp_dev((t + i) % TP) for i in range(1, TP)]
    for dev in greet:
        pl.semaphore_signal(barrier, inc=1, device_id=dev, device_id_type=MESH)

    @pl.when(mid)
    def _():
        pl.semaphore_signal(barrier, inc=1, device_id=z_dev(3 - p), device_id_type=MESH)

    eye = lax.broadcasted_iota(jnp.int32, (HD, HD), 0) == lax.broadcasted_iota(jnp.int32, (HD, HD), 1)
    pl.semaphore_wait(barrier, len(greet) + inner)

    pending = []

    def go(copy):
        copy.start()
        pending.append(copy)

    def hid_ref(holder, half):
        if half is None:
            return hbuf.at[holder]
        return hbuf.at[holder, pl.ds(half * (FEAT // 2), FEAT // 2)]

    def hid_copy(i, holder, half, dev):
        ref = hid_ref(holder, half)
        go(copy_to(ref, ref, hs.at[i], hr.at[i], tp_dev(dev)))

    def hid_wait(i, holder, half):
        ref = hid_ref(holder, half)
        copy_to(ref, ref, hs.at[i], hr.at[i], tp_dev(t)).wait_recv()

    def sq_copy(i):
        return copy_to(sq.at[t], sq.at[t], qss.at[i], qsr.at[i], tp_dev((t + i) % TP))

    def sq_wait(i):
        ref = sq.at[(t + TP - i) % TP]
        copy_to(ref, ref, qss.at[i], qsr.at[i], tp_dev(t)).wait_recv()

    def scatter(h, rel):
        slot = slot_at(rel)
        src = kvs.at[h, pl.ds(pl.multiple_of(slot * SL, SL), SL)]
        return copy_to(src, kvb[h].at[me], cs.at[h, rel], cr.at[h, rel], row_dev(slot))

    def scatter_wait(h, rel):
        ref = kvb[h].at[p * 8 + slot_at(8 - rel)]
        copy_to(ref, ref, cs.at[h, rel], cr.at[h, rel], row_dev(s)).wait_recv()

    def z_rows(h, z):
        return kvb[h].at[pl.ds(pl.multiple_of(z * 8, 8), 8)]

    def z_copy(h, k, which):
        if which == "first":
            ref, target, sem, at = z_rows(h, p), zo[0], 0, 0
        elif which == "second":
            ref, target, sem, at = z_rows(h, p), 3 - p, 1, 1
        else:
            ref, target, sem = z_rows(h, zo[k]), (3 - p if k == 0 else 3 * p - 3), 2 + k
            at = (2, 1, 2)[k]
        return copy_to(ref, ref, zs.at[h, sem], zr.at[h, at], z_dev(target))

    def z_own(h):
        go(z_copy(h, 0, "first"))

        @pl.when(mid)
        def _():
            z_copy(h, 0, "second").start()

    def z_wait(h, k):
        ref = z_rows(h, zo[k])
        copy_to(ref, ref, zs.at[h, 0], zr.at[h, k], z_dev(p)).wait_recv()

    def z_relay(h, *ks):
        @pl.when(mid)
        def _():
            for k in ks:
                z_wait(h, k)
                z_copy(h, k, "relay").start()

    def z_take(h):
        @pl.when(inner == 0)
        def _():
            for k in range(3):
                z_wait(h, k)

    def project(holder, row_scale):
        at = pl.ds(pl.multiple_of(holder * FEAT, FEAT), FEAT)
        gain = gcol[at, :]
        normed = hbuf[holder].astype(F32) * row_scale * jnp.concatenate([gain, gain], axis=1)
        acc[...] += lax.dot_general(
            normed.astype(BF), wbuf[at, :], (((0,), (0,)), ((), ())), preferred_element_type=F32
        )

    for half in range(2):
        src = hid.at[pl.ds(half * (FEAT // 2), FEAT // 2)]
        go(copy_to(src, hid_ref(t, half), hs.at[half], hr.at[half], tp_dev(there + y)))
    go(copy_to(hid, hid_ref(t, None), hs.at[2], hr.at[2], tp_dev(here + yp)))
    go(copy_to(hid, hid_ref(t, None), hs.at[3], hr.at[3], tp_dev(here + ym)))
    own_hid.wait()
    features = hbuf[t].astype(F32)
    sq[t] = jnp.broadcast_to(jnp.sum(features * features, axis=0, keepdims=True), (8, ROWS))
    own_kv.wait()
    for h in range(2):
        kf32[...] = kraw[:, :, h * HD : (h + 1) * HD].astype(F32).reshape(1024, HD)
        kvs[h, :, :HD] = kf32[pl.ds(0, 512, stride=2), :].astype(BF)
        kvs[h, :, HD:] = kf32[pl.ds(1, 512, stride=2), :].astype(BF)
    for h in range(2):
        kvb[h][me] = kvs[h, pl.ds(pl.multiple_of(s * SL, SL), SL), :]
    for i in range(1, TP):
        go(sq_copy(i))
    for h in range(2):
        for rel in range(1, 8):
            go(scatter(h, rel))

    acc[...] = jnp.zeros_like(acc)
    for load in tables:
        load.wait()
    vscr[...] = jnp.ones_like(vscr)
    for i in range(TP * FEAT // HD):
        at = slice(i * HD, (i + 1) * HD)
        spread = jnp.where(eye, jnp.broadcast_to(gain_ref[at].reshape(1, HD), (HD, HD)), 0.0)
        gcol[at, :] = jnp.broadcast_to(jnp.sum(spread, axis=1, keepdims=True), (HD, HD))

    def scatter_waits(h):
        for rel in range(1, 8):
            scatter_wait(h, rel)

    scatter_waits(0)
    z_own(0)
    hid_wait(2, here + ym, None)
    hid_copy(4, here + ym, 0, here + yp)
    hid_wait(3, here + yp, None)
    hid_copy(5, here + yp, 1, here + ym)
    hid_wait(0, there + y, 0)
    hid_copy(6, there + y, 0, here + yp)
    hid_copy(7, there + y, 0, here + ym)
    scatter_waits(1)
    z_own(1)
    for i in range(1, TP):
        sq_wait(i)
    total = sq[0]
    for i in range(1, TP):
        total = total + sq[i]
    row_scale = lax.rsqrt(total[0:1, :] / (TP * FEAT) + 1e-6)
    for load in loads:
        load.wait()
    project(t, row_scale)
    project(here + ym, row_scale)
    hid_wait(6, there + ym, 0)
    hid_copy(10, there + ym, 0, here + yp)
    project(here + yp, row_scale)
    hid_wait(1, there + y, 1)
    hid_copy(8, there + y, 1, here + yp)
    hid_copy(9, there + y, 1, here + ym)
    z_relay(0, 0, 1)
    hid_wait(4, here + yq, 0)
    hid_wait(5, here + yq, 1)
    project(here + yq, row_scale)
    project(there + y, row_scale)
    hid_wait(9, there + yp, 1)
    hid_copy(11, there + yp, 1, here + ym)
    hid_wait(8, there + ym, 1)
    project(there + ym, row_scale)
    hid_wait(7, there + yp, 0)
    project(there + yp, row_scale)
    hid_wait(10, there + yq, 0)
    hid_wait(11, there + yq, 1)
    project(there + yq, row_scale)

    cosine, sine = cos_ref[...], sin_ref[...]
    live = lax.broadcasted_iota(jnp.int32, (ROWS, HD), 0) < length_ref[me]

    def rotated(at):
        v = acc[:, at : at + HD]
        return v * cosine + pltpu.roll(v, 64, 1) * sine

    def q_copy(h, slot, sem, rel, dev):
        ref = qb[h].at[slot]
        return copy_to(ref, ref, qs.at[h, sem], qr.at[h, rel], dev)

    def q_wait(h, rel):
        ref = qb[h].at[slot_at(rel)]
        copy_to(ref, ref, qs.at[h, 0], qr.at[h, rel], row_dev(s)).wait_recv()

    def sib_rel(rel):
        return (rel + 2 * c + 7) % 8

    def weigh(scores):
        return jnp.exp2(jnp.tanh(scores * (1.0 / 50.0)) * (50.0 * LOG2E))

    contract = (((1,), (1,)), ((), ()))
    for h in range(2):
        for g in range(2):
            q = (rotated((2 * h + g) * HD) * (1.0 / 12.0)).astype(BF)
            qb[h][s, g * ROWS : (g + 1) * ROWS, :] = q
    for h in range(2):
        key_ref[:, h * HD : (h + 1) * HD] = jnp.where(live, rotated(512 + h * HD), 0.0).astype(BF)
        v = acc[:, 768 + h * HD : 768 + (h + 1) * HD]
        val_ref[:, h * HD : (h + 1) * HD] = jnp.where(live, v, 0.0).astype(BF)
        for n, rel in enumerate((2, 6, 4)):
            go(q_copy(h, s, n, 8 - rel, row_dev(slot_at(rel))))
        go(q_copy(h, s, 3, sib_rel(0), (sibling, t)))
    row_id = lax.broadcasted_iota(jnp.int32, (2 * ROWS, ROWS), 0) % ROWS
    col_id = lax.broadcasted_iota(jnp.int32, (2 * ROWS, ROWS), 1)
    causal = row_id >= col_id
    ones = jnp.ones((ROWS, HD), BF)
    for h in range(2):
        scores = lax.dot_general(
            qb[h][s], key_ref[:, h * HD : (h + 1) * HD], contract, preferred_element_type=F32
        )
        w = jnp.where(causal, weigh(scores), 0.0).astype(BF)
        values = jnp.concatenate([val_ref[:, h * HD : (h + 1) * HD], ones], axis=1)
        both = jnp.dot(w, values, preferred_element_type=F32)
        snum[h] = both[:, :HD]
        sden[h] = both[:, HD:]

    def q_forward(h):
        for n, rel in enumerate((2, 6, 4)):
            q_wait(h, rel)
            go(q_copy(h, slot_at(rel), 4 + n, sib_rel(rel), (sibling, t)))

    def q_rest(h):
        for rel in (1, 3, 5, 7):
            q_wait(h, rel)

    def num_copy(h, i, dev):
        return copy_to(ns[h].at[i], nl[h].at[i], rs.at[h, i], rr.at[h, i], dev)

    def den_copy(h, i, dev):
        return copy_to(ds[h].at[i], dl[h].at[i], es.at[h, i], er.at[h, i], dev)

    def land_wait(h, i):
        num_copy(h, i, row_dev(s)).wait_recv()
        den_copy(h, i, row_dev(s)).wait_recv()

    def attend_loop(h, first, last):
        @pl.loop(first, last)
        def _(n):
            third, rest = n // 3, n % 3
            shuffled = 1 - rest + (rest // 2) * 3 + 4 * third
            i = (1 - third // 2) * shuffled + (third // 2) * (3 + 4 * rest)
            dx = (i + 1) % 4
            core = (1 - c) + (i // 4) * (2 * c - 1)
            slot = ((x + dx) % 4) * 2 + core
            group = group_ref[p * 8 + slot]
            for j in range(8):
                block = kvb[h][owner_ref[group, j]]
                kscr[j * SL : (j + 1) * SL, :] = block[:, :HD]
                vscr[j * SL : (j + 1) * SL, :HD] = block[:, HD:]
            scores = lax.dot_general(qb[h][slot], kscr[...], contract, preferred_element_type=F32)
            both = jnp.dot(weigh(scores).astype(BF), vscr[...], preferred_element_type=F32)

            @pl.when(i < 7)
            def _():
                num = both[:, :HD]
                for g in range(4):
                    den = both[g * HD : (g + 1) * HD, HD:]
                    ds[h][i, g : g + 1, :] = jnp.sum(jnp.where(eye, den, 0.0), axis=0, keepdims=True)

                @pl.when(i < 4)
                def _():
                    ns[h][i] = num.astype(BF)
                    num_copy(h, i, (sibling, t)).start()
                    den_copy(h, i, (sibling, t)).start()

                @pl.when(i >= 4)
                def _():
                    land_wait(h, i - 4)
                    ns[h][i] = (num + nl[h][i - 4].astype(F32)).astype(BF)
                    ds[h][i] = ds[h][i] + dl[h][i - 4]
                    num_copy(h, i, row_dev(slot)).start()
                    den_copy(h, i, row_dev(slot)).start()

            @pl.when(i == 7)
            def _():
                snum[h] += both[:, :HD]
                sden[h] += both[:, HD:]

    def combine(h):
        for i in range(3, 7):
            land_wait(h, i)
        den_rows = dl[h][3] + dl[h][4] + dl[h][5] + dl[h][6]
        for g in range(4):
            at = slice(g * HD, (g + 1) * HD)
            spread = jnp.where(eye, jnp.broadcast_to(den_rows[g : g + 1, :], (HD, HD)), 0.0)
            den = jnp.sum(spread, axis=1, keepdims=True) + sden[h, at, :]
            num = snum[h, at, :]
            for i in range(3, 7):
                num = num + nl[h][i, at, :].astype(F32)
            r0 = (g % 2) * HD
            head = 2 * h + g // 2
            rows_live = (lax.broadcasted_iota(jnp.int32, (HD, HD), 0) + r0) < length_ref[me]
            out = jnp.where(rows_live, num / den, 0.0).astype(BF)
            att_ref[r0 : r0 + HD, head * HD : (head + 1) * HD] = out

    z_relay(0, 2)
    z_relay(1, 0, 1)
    q_forward(0)
    q_rest(0)
    z_take(0)
    attend_loop(0, 0, 4)
    q_forward(1)
    z_relay(1, 2)
    attend_loop(0, 4, 8)
    q_rest(1)
    combine(0)
    z_take(1)
    attend_loop(1, 0, 8)
    combine(1)

    for copy in pending:
        copy.wait_send()
    for h in range(2):
        for i in range(7):
            num_copy(h, i, row_dev(s)).wait_send()
            den_copy(h, i, row_dev(s)).wait_send()

    @pl.when(mid)
    def _():
        for h in range(2):
            z_copy(h, 0, "second").wait_send()
            for k in range(3):
                z_copy(h, k, "relay").wait_send()


def finish(att, key, val, att_out, key_out, val_out):
    att_out[...] = att[...]
    key_out[...] = key[...]
    val_out[...] = val[...]


def body(hidden, norm_gain, w_query, w_key, w_value, prefix_kv, group_of, block_owner, lengths):
    full_cos, signed_sin = rope_constants()
    smem = pl.BlockSpec(memory_space=pltpu.SMEM)
    vmem = pl.BlockSpec(memory_space=pltpu.VMEM)
    hbm = pl.BlockSpec(memory_space=pl.ANY)
    dma = pltpu.SemaphoreType.DMA
    pair = lambda shape, dtype: [pltpu.VMEM(shape, dtype)] * 2
    shapes = tuple(jax.ShapeDtypeStruct((ROWS, n), BF) for n in (512, 256, 256))
    results = pl.pallas_call(
        kernel,
        out_shape=tuple(pltpu.VMEM((ROWS, n), BF) for n in (512, 256, 256)),
        in_specs=[smem] * 3 + [hbm] * 8,
        out_specs=(vmem, vmem, vmem),
        scratch_shapes=[
            pltpu.VMEM((TP * FEAT,), F32),
            pltpu.VMEM((ROWS, HD), F32),
            pltpu.VMEM((ROWS, HD), F32),
            pltpu.VMEM((TP, FEAT, ROWS), BF),
            pltpu.VMEM((TP * FEAT, 1024), BF),
            pltpu.VMEM((512, 2, 256), BF),
            pltpu.VMEM((1024, HD), F32),
            pltpu.VMEM((2, 512, 256), BF),
            *pair((32, SL, 256), BF),
            *pair((8, 512, HD), BF),
            *pair((8, 512, HD), BF),
            *pair((8, 512, HD), BF),
            *pair((8, 8, HD), F32),
            *pair((8, 8, HD), F32),
            pltpu.VMEM((ROWS, 1024), F32),
            pltpu.VMEM((TP, 8, ROWS), F32),
            pltpu.VMEM((TP * FEAT, HD), F32),
            pltpu.VMEM((512, HD), BF),
            pltpu.VMEM((512, 2 * HD), BF),
            pltpu.VMEM((2, 512, HD), F32),
            pltpu.VMEM((2, 512, HD), F32),
            dma((5,)), dma((3,)), dma((8,)), dma((8,)), dma((12,)), dma((12,)),
            dma((2, 8)), dma((2, 8)), dma((2, 5)), dma((2, 3)),
            dma((2, 8)), dma((2, 8)), dma((2, 8)), dma((2, 8)), dma((2, 8)), dma((2, 8)),
        ],
        name="prefill",
        compiler_params=pltpu.CompilerParams(
            collective_id=1, has_side_effects=True, vmem_limit_bytes=56 * 2**20
        ),
    )(
        group_of, block_owner, lengths, hidden.T, w_query, w_key, w_value, prefix_kv, norm_gain,
        jnp.asarray(full_cos), jnp.asarray(signed_sin),
    )
    return pl.pallas_call(
        finish, out_shape=shapes, in_specs=[vmem] * 3, out_specs=(vmem, vmem, vmem), name="finish",
        compiler_params=pltpu.CompilerParams(vmem_limit_bytes=4 * 2**20),
    )(*results)


def solution(mesh):
    in_specs = (
        P("req", "tp"), P(), P(None, "tp"), P(None, "tp"), P(None, "tp"),
        P("req", None, "tp"), P(), P(), P(),
    )
    out_specs = (P("req", "tp"), P("req", "tp"), P("req", "tp"))
    return jax.shard_map(body, mesh=mesh, in_specs=in_specs, out_specs=out_specs, check_vma=False)
```
